32 devices in a mesh: tiles: 16 (over z, y, x), depth: 2 (over core).
Axes of the slice: x: 2, y: 2, z: 4, core: 2. Of those that a mesh axis runs over, the one named last changes fastest.
Arguments:
- momentum: float32 [16, 16, 6300], P('tiles', 'depth'), may hold values from -6 to 6
- tracer: float32 [16, 16, 6300], P('tiles', 'depth'), may hold values from -6 to 6
- mom_diffusivity: float32 [16, 16, 6300], P('tiles', 'depth'), may hold values from 0.02 to 0.2
- tra_diffusivity: float32 [16, 16, 6300], P('tiles', 'depth'), may hold values from 0.02 to 0.2
- mixing: float32 [16, 16, 6300], P('tiles', 'depth'), may hold values from 0.05 to 0.4
- wet_mask: int32 [16, 6300], P('tiles'), may hold values 0 or 1
- neighbours: int32 [16, 4], P('tiles'), may hold values from -1 to 15, as said below
- source_edges: int32 [16, 4], P('tiles'), may hold values from 0 to 3, as said below
- flips: int32 [16, 4], P('tiles'), may hold values from 0 to 1
- mom_cotangent: float32 [16, 16, 6300], P('tiles', 'depth'), may hold values from -6 to 6
- tra_cotangent: float32 [16, 16, 6300], P('tiles', 'depth'), may hold values from -6 to 6
Outputs:
- final_momentum: float32 [16, 16, 6300], P('tiles', 'depth')
- final_tracer: float32 [16, 16, 6300], P('tiles', 'depth')
- grad_momentum: float32 [16, 16, 6300], P('tiles', 'depth')
- grad_tracer: float32 [16, 16, 6300], P('tiles', 'depth')
The draws below stay inside these ranges and needn't reach their ends.
Inputs may be any that keep to these rules, and one draw needn't show every extreme that they name: `neighbours`: the neighbour relation is symmetric, also across the fold seam, where a tile's north edge faces another tile's north edge in reverse order; -1 marks a missing neighbour. `source_edges`: for north and south directions the facing edge is north or south, for east and west directions it is east or west.
All inputs are finite; a program needn't handle non-finite values. No bound on the sum of `wet_mask` on one device may be relied on, other than what follows from the above.
Results may differ from the reference program's by a relative error of at most 0.00002.
Values sent between devices are 32-bit elements; how exact they have to be, the bound alone decides.
A program may use at most 64 MiB of HBM per device.

```python
import math
import jax
import jax.numpy as jnp

NI = 90
NJ = 70
TILES_ALL = 16
LEVELS = 16
CELLS = 6300


grid_columns = 8


def topology(key):
    order = jax.random.permutation(jax.random.fold_in(key, 11), TILES_ALL).astype(jnp.int32)
    position = jnp.zeros((TILES_ALL,), jnp.int32).at[order].set(jnp.arange(TILES_ALL, dtype=jnp.int32))
    column = position % grid_columns
    row = position // grid_columns
    rows_all = TILES_ALL // grid_columns
    at_top = row == rows_all - 1
    at_bottom = row == 0
    north_pos = jnp.where(at_top, row * grid_columns + (grid_columns - 1 - column), position + grid_columns)
    south_pos = jnp.clip(position - grid_columns, 0, TILES_ALL - 1)
    east_pos = row * grid_columns + (column + 1) % grid_columns
    west_pos = row * grid_columns + (column + grid_columns - 1) % grid_columns
    north_pos = jnp.clip(north_pos, 0, TILES_ALL - 1)
    found = jnp.stack([order[north_pos], jnp.where(at_bottom, -1, order[south_pos]), order[east_pos], order[west_pos]], axis=1)
    zeros_col = jnp.zeros((TILES_ALL,), jnp.int32)
    facing_edge = jnp.stack([jnp.where(at_top, 0, 1).astype(jnp.int32), zeros_col, zeros_col + 3, zeros_col + 2], axis=1)
    reversed_flag = jnp.stack([at_top.astype(jnp.int32), zeros_col, zeros_col, zeros_col], axis=1)
    return (found.astype(jnp.int32), facing_edge, reversed_flag)


def draw_neighbours(key, part):
    return topology(key)[0]


def draw_source_edges(key, part):
    return topology(key)[1]


def draw_flips(key, part):
    return topology(key)[2]


def touch_ends(drawn, own_key, smallest, high):
    longest = drawn.shape.index(max(drawn.shape))
    spots = []
    for shift in (0, 1):
        where = [jax.random.randint(jax.random.fold_in(own_key, axis), (), 0, length) for axis, length in enumerate(drawn.shape)]
        where[longest] = (where[longest] + shift) % drawn.shape[longest]
        spots.append(tuple(where))
    return drawn.at[spots[0]].set(smallest).at[spots[1]].set(high)


def level_of(stream_key, shape, pieces, least, high):
    level, own = 1.0, jax.random.fold_in(stream_key, 6)
    for dim, shards_of in pieces:
        heights = jnp.exp(jax.random.uniform(jax.random.fold_in(own, dim), (shards_of,), jnp.float32, least / len(pieces), high / len(pieces)))
        level = level * jnp.repeat(heights, shape[dim] // shards_of).reshape([-1 if axis == dim else 1 for axis in range(len(shape))])
    return level


def bell_draw(key, extent, scale, bound, pieces=(), held_as=jnp.bfloat16):
    loudness = level_of(key, extent, pieces, -0.22, 0.18) if pieces else 1.0
    result = jax.random.normal(key, extent, jnp.float32) * scale * loudness
    return jnp.minimum(jnp.maximum(result, -bound), bound).astype(held_as)


def setup_inputs(seed: int = 0) -> dict:
    streams_of = jax.random.split(jax.random.key(seed), 12)
    return {
        "momentum": bell_draw(streams_of[0], (TILES_ALL, LEVELS, CELLS), 1.0, 6.0, ((0, 16), (1, 2)), jnp.float32),
        "tracer": bell_draw(streams_of[1], (TILES_ALL, LEVELS, CELLS), 1.0, 6.0, ((0, 16), (1, 2)), jnp.float32),
        "mom_diffusivity": jnp.clip(jnp.exp(math.log(0.2) - 2.3025851 * jax.random.uniform(streams_of[2], (TILES_ALL, LEVELS, CELLS), jnp.float32) ** level_of(streams_of[2], (TILES_ALL, LEVELS, CELLS), ((0, 16), (1, 2)), -0.2, 0.2)), 0.02, 0.2),
        "tra_diffusivity": jnp.clip(jnp.exp(math.log(0.2) - 2.3025851 * jax.random.uniform(streams_of[3], (TILES_ALL, LEVELS, CELLS), jnp.float32) ** level_of(streams_of[3], (TILES_ALL, LEVELS, CELLS), ((0, 16), (1, 2)), -0.2, 0.2)), 0.02, 0.2),
        "mixing": jnp.clip(jnp.exp(math.log(0.4) - 2.0794415 * jax.random.uniform(streams_of[4], (TILES_ALL, LEVELS, CELLS), jnp.float32) ** level_of(streams_of[4], (TILES_ALL, LEVELS, CELLS), ((0, 16), (1, 2)), -0.2, 0.2)), 0.05, 0.4),
        "wet_mask": touch_ends((jax.random.randint(streams_of[5], (TILES_ALL, CELLS), 0, 4) < 3).astype(jnp.int32), jax.random.fold_in(streams_of[5], 1), 0, 1),
        "neighbours": draw_neighbours(jax.random.fold_in(streams_of[11], 71), 0),
        "source_edges": draw_source_edges(jax.random.fold_in(streams_of[11], 71), 0),
        "flips": draw_flips(jax.random.fold_in(streams_of[11], 71), 0),
        "mom_cotangent": bell_draw(streams_of[9], (TILES_ALL, LEVELS, CELLS), 1.0, 6.0, ((0, 16), (1, 2)), jnp.float32),
        "tra_cotangent": bell_draw(streams_of[10], (TILES_ALL, LEVELS, CELLS), 1.0, 6.0, ((0, 16), (1, 2)), jnp.float32),
    }


def edges_of(field):
    total = field.shape[-1]
    return jnp.concatenate([field[..., total - NI:], field[..., :NI], field[..., NI - 1::NI], field[..., ::NI]], axis=-1)

def pick_edge(chosen, source, flip, direction):
    if direction < 2:
        strip = jnp.where(source[:, None, None] == 0, chosen[..., :NI], chosen[..., NI:2 * NI])
    else:
        strip = jnp.where(source[:, None, None] == 2, chosen[..., 2 * NI:2 * NI + NJ], chosen[..., 2 * NI + NJ:])
    return jnp.where(flip[:, None, None] == 1, strip[..., ::-1], strip)

def facing(edge_all, neighbours, source_edges, flips):
    strips = []
    for direction in range(4):
        target = neighbours[:, direction]
        row_index = jnp.clip(target, 0, edge_all.shape[0] - 1).astype(jnp.int32)
        chosen = jnp.take(edge_all, row_index, axis=0)
        strip = pick_edge(chosen, source_edges[:, direction], flips[:, direction], direction)
        strips.append(jnp.where((target >= 0)[:, None, None], strip, jnp.zeros_like(strip)))
    return jnp.concatenate(strips, axis=-1)

def shifted_sum(values, halo):
    total = values.shape[-1]
    column = jnp.arange(total) % NI
    north = jnp.concatenate([values[..., NI:], halo[..., :NI]], axis=-1)
    south = jnp.concatenate([halo[..., NI:2 * NI], values[..., :total - NI]], axis=-1)
    east_halo = jnp.repeat(halo[..., 2 * NI:2 * NI + NJ], NI, axis=-1)
    west_halo = jnp.repeat(halo[..., 2 * NI + NJ:], NI, axis=-1)
    east = jnp.where(column == NI - 1, east_halo, jnp.concatenate([values[..., 1:], values[..., :1]], axis=-1))
    west = jnp.where(column == 0, west_halo, jnp.concatenate([values[..., -1:], values[..., :-1]], axis=-1))
    return north + south + east + west

def laplace(field, weighted_halo, wet, wet_halo):
    values = shifted_sum(wet * field, weighted_halo)
    weights = shifted_sum(wet, wet_halo)
    return wet * (values - weights * field)

def vertical(field):
    zeros_level = jnp.zeros_like(field[:, :1])
    above = jnp.concatenate([zeros_level, field[:, :-1]], axis=1)
    below = jnp.concatenate([field[:, 1:], zeros_level], axis=1)
    level_index = jnp.arange(field.shape[1])
    has_above = (level_index > 0).astype(jnp.float32)[None, :, None]
    has_below = (level_index < field.shape[1] - 1).astype(jnp.float32)[None, :, None]
    return has_above * (above - field) + has_below * (below - field)

def reference(momentum, tracer, mom_diffusivity, tra_diffusivity, mixing, wet_mask, neighbours, source_edges, flips, mom_cotangent, tra_cotangent):
    wet = wet_mask[:, None, :].astype(jnp.float32)
    wet_halo = facing(edges_of(wet_mask[:, None, :]), neighbours, source_edges, flips).astype(jnp.float32)
    press_scale = LEVELS ** (-0.5)

    def operator(field):
        halo = facing(edges_of(field), neighbours, source_edges, flips)
        return laplace(field, wet_halo * halo, wet, wet_halo)

    def forward_step(state):
        mom_now, tra_now = state
        press = press_scale * jnp.cumsum(tra_now, axis=1)
        mom_next = mom_now + mom_diffusivity * operator(mom_now) - 0.1 * operator(press)
        tra_next = tra_now + tra_diffusivity * operator(tra_now) + mixing * vertical(tra_now) + 0.2 * mom_now
        return (mom_next, tra_next)

    def two_steps(mom_start, tra_start):
        return forward_step(forward_step((mom_start, tra_start)))
    finals, pullback = jax.vjp(two_steps, momentum, tracer)
    grads = pullback((mom_cotangent, tra_cotangent))
    return (finals[0], finals[1], grads[0], grads[1])
```

```python
import functools

import jax
import jax.numpy as jnp
from jax import lax
from jax.experimental import pallas as pl
from jax.experimental.pallas import tpu as pltpu
from jax.sharding import PartitionSpec as P

NI = 90
NJ = 70
CELLS = NI * NJ
LANES = 128
MAIN = 64 * NI
BLOCK = 5 * LANES
BLOCKS = MAIN // BLOCK
WIDTH = MAIN + BLOCK
REST = CELLS - MAIN
GRID = WIDTH + 2 * LANES
NORTH = NI * (NJ - 1) % LANES
HEAD = LANES - NI
SIX = NJ - 64
INVERSE = 37
MESH = pl.DeviceIdType.MESH


def roll(x, shift, axis=1):
    return pltpu.roll(x, shift % x.shape[axis], axis)


def pick(x, lanes):
    return jnp.take_along_axis(x, lanes & (LANES - 1), axis=1, mode="promise_in_bounds")


def kernel(
    inner, outer, depth, levels_all,
    mom_hbm, tra_hbm, mdif_hbm, tdif_hbm, mix_hbm, wet_hbm, nb_hbm, se_hbm, fl_hbm, mcot_hbm, tcot_hbm,
    mom_out, tra_out, mgrad_out, tgrad_out,
    mom_ref, tra_ref, mdif_ref, tdif_ref, mix_ref, wet_ref, nb_ref, se_ref, fl_ref, mcot_ref, tcot_ref,
    fl_s, on_ref, ke_ref, kw_ref, wet8, grid, base, edge_s, edge_r,
    a_s, b_s, m_s, ga_0, ga_1, gb_0, gb_1, gm_0, gm_1, ha_s, hb_s, hm_s, ha_r, hb_r, hm_r,
    table, tables, tables_s,
    in_sem, fl_sem, tab_send, tab_recv, tab_local, e_send, e_recv,
    a1_send, a1_recv, b1_send, b1_recv, m1_send, m1_recv,
    a2_send, a2_recv, b2_send, b2_recv, m2_send, m2_recv,
):
    me = lax.axis_index("tiles")
    d = lax.axis_index("depth")
    member = lax.rem(me, inner)
    group = lax.div(me, inner)
    relay = depth - 1 - d
    rows = mom_ref.shape[1]
    press = -0.1 * levels_all ** (-0.5)
    f32 = jnp.float32

    def in_inner(o, at):
        return {"tiles": group * inner + lax.rem(member + o, inner), "depth": at}

    def in_outer(o, at):
        return {"tiles": lax.rem(group + o, outer) * inner + member, "depth": at}

    def shifted(o):
        return lax.rem(d + o, depth)

    small = pltpu.make_async_copy(fl_hbm, fl_s, fl_sem)
    small.start()
    fetched = []
    for k, (src, dst) in enumerate((
        (nb_hbm, nb_ref), (se_hbm, se_ref), (wet_hbm, wet_ref), (mom_hbm, mom_ref), (tra_hbm, tra_ref),
        (mcot_hbm, mcot_ref), (tcot_hbm, tcot_ref), (mdif_hbm, mdif_ref), (tdif_hbm, tdif_ref), (mix_hbm, mix_ref),
    )):
        fetched.append(pltpu.make_async_copy(src, dst, in_sem.at[k]))
        fetched[-1].start()
    barrier = pltpu.get_barrier_semaphore()
    greeted = [in_inner(o, at) for o in range(1, inner) for at in (d, relay)]
    greeted += [in_outer(o, shifted(k)) for o in range(outer) for k in range(1, depth)]
    for device in greeted:
        pl.semaphore_signal(barrier, inc=1, device_id=device, device_id_type=MESH)

    started = []

    def send(src, dst, ssem, rsem, to):
        copy = pltpu.make_async_remote_copy(
            src_ref=src, dst_ref=dst, send_sem=ssem, recv_sem=rsem, device_id=to, device_id_type=MESH
        )
        copy.start()
        started.append(copy)
        return copy

    lane = lax.broadcasted_iota(jnp.int32, (rows, LANES), 1)
    sub = lax.broadcasted_iota(jnp.int32, (rows, LANES), 0)
    level = lax.broadcasted_iota(jnp.int32, (rows, BLOCK), 0)
    place = lax.broadcasted_iota(jnp.int32, (rows, BLOCK), 1).astype(f32)
    odd = (lane & 1) == 1
    i_n = (lane + LANES - NORTH) & (LANES - 1)
    i_s = lane
    j_m = (jnp.where(odd, (lane + LANES - NI + 1) >> 1, lane >> 1) * INVERSE) & 63
    j_t = jnp.full_like(lane, -1)
    for j in range(64, NJ):
        for x in (NI * j % LANES, (NI * j + NI - 1) % LANES):
            j_t = jnp.where(lane == x, j, j_t)
    is_t = j_t >= 0
    corner_s = (lane == 0) | (lane == NI - 1)
    corner_n = (lane == NORTH) | (lane == (NORTH + NI - 1) % LANES)

    zero = jnp.zeros((5 * rows, LANES), f32)
    grid[:, 0:LANES] = zero
    grid[:, GRID - 2 * LANES : GRID - LANES] = zero
    grid[:, GRID - LANES :] = zero
    table[...] = jnp.zeros_like(table)

    def marks(b, carry):
        lo = pl.multiple_of(b * BLOCK, LANES)
        pos = place + lo.astype(f32)
        col = pos - NI * jnp.floor((pos + 0.5) * (1.0 / NI))
        inside = pos < CELLS - 0.5
        west = (col < 0.5) & inside
        east = (col > NI - 1.5) & inside
        on_ref[:, pl.ds(lo, BLOCK)] = jnp.where(west | east, 1.0, 0.0)
        ke_ref[:, pl.ds(lo, BLOCK)] = jnp.where(east, 0.0, 1.0)
        kw_ref[:, pl.ds(lo, BLOCK)] = jnp.where(west, 0.0, 1.0)
        return carry

    lax.fori_loop(0, BLOCKS + 1, marks, 0)

    small.wait()
    for copy in fetched[:2]:
        copy.wait()
    table[0:1, 0:4] = nb_ref[...]
    table[1:2, 0:4] = se_ref[...]
    flip = [fl_s[0, k] for k in range(4)]
    f_ew = jnp.where(odd, flip[2], flip[3])
    i_n = i_n + flip[0] * (NI - 1 - 2 * i_n)
    i_s = i_s + flip[1] * (NI - 1 - 2 * i_s)
    j_m = j_m + f_ew * (NJ - 1 - 2 * j_m)
    j_t = j_t + f_ew * (NJ - 1 - 2 * j_t)
    m_main, t_main = j_m < 64, j_t < 64
    shift = jnp.where(odd, 0, NI - 1)
    m_from, t_from = NI * j_m + shift, NI * j_t + shift
    shift = jnp.where(odd, NI - HEAD, LANES - 2 * SIX) - 64
    m_rest, t_rest = j_m + shift, j_t + shift

    for copy in fetched[2:]:
        copy.wait()

    def padded(x):
        return jnp.concatenate([x, jnp.zeros((x.shape[0], BLOCK - REST), x.dtype)], axis=1)

    def field(ref):
        def load(lo, last):
            return padded(ref[0, :, MAIN:CELLS]) if last else ref[0, :, pl.ds(lo, BLOCK)]
        return load

    def kept(k):
        def load(lo, last):
            return base[k, :, MAIN:WIDTH] if last else base[k, :, pl.ds(lo, BLOCK)]
        return load

    def wide(ref):
        def load(lo, last):
            return ref[:, MAIN:WIDTH] if last else ref[:, pl.ds(lo, BLOCK)]
        return load

    def wet_int(lo, last):
        x = padded(wet_ref[0:1, MAIN:CELLS]) if last else wet_ref[0:1, pl.ds(lo, BLOCK)]
        return jnp.broadcast_to(x.astype(f32), (rows, BLOCK))

    mdif, tdif, mix = field(mdif_ref), field(tdif_ref), field(mix_ref)
    on, keep_e, keep_w, wet_at = wide(on_ref), wide(ke_ref), wide(kw_ref), wide(wet8)

    def cut(x, c):
        return x[:, c * LANES : (c + 1) * LANES]

    def collect(acc, x, mask):
        for c in range(BLOCK // LANES):
            acc = jnp.where(cut(mask, c) > 0.5, cut(x, c), acc)
        return acc

    def sweep(body, count):
        def step(b, accs):
            lo = pl.multiple_of(b * BLOCK, LANES)
            mask = on(lo, False)
            return tuple(collect(a, x, mask) for a, x in zip(accs, body(lo, False)))
        accs = lax.fori_loop(0, BLOCKS, step, (jnp.zeros((rows, LANES), f32),) * count)
        mask = on(MAIN, True)
        ends = body(MAIN, True)
        tails = [collect(jnp.zeros((rows, LANES), f32), x, mask) for x in ends]
        norths = [jnp.where(lane >= NORTH, cut(x, 3), cut(x, 4)) for x in ends]
        return norths, accs, tails

    def running(x, down):
        at = lax.broadcasted_iota(jnp.int32, x.shape, 0)
        k = 1
        while k < rows:
            if down:
                x = x + jnp.where(at >= k, roll(x, k, 0), 0.0)
            else:
                x = x + jnp.where(at < rows - k, roll(x, rows - k, 0), 0.0)
            k *= 2
        return x

    def total(x):
        k = rows // 2
        while k >= 1:
            x = x + roll(x, k, 0)
            k //= 2
        return x

    sources = [field(r) for r in (mom_ref, tra_ref, mcot_ref, tcot_ref, mdif_ref, tdif_ref)]

    def first_body(lo, last):
        w = wet_int(lo, last)
        if last:
            wet8[:, MAIN:WIDTH] = w
        else:
            wet8[:, pl.ds(lo, BLOCK)] = w
        return [load(lo, last) for load in sources] + [w]

    norths, accs, tails = sweep(first_body, 7)
    souths = [r[0, :, 0:LANES] for r in (mom_ref, tra_ref, mcot_ref, tcot_ref, mdif_ref, tdif_ref)] + [wet8[:, 0:LANES]]
    packs = [list(p) for p in zip(norths, souths, accs, tails)]
    state = packs[:4]
    mdif_p, tdif_p, wet_p = packs[4:]
    wet_p[0] = jnp.where((lane >= NORTH) | (lane < NORTH + NI - LANES), wet_p[0], 0.0)
    wet_p[1] = jnp.where(lane < NI, wet_p[1], 0.0)
    wet_p[3] = jnp.where(is_t, wet_p[3], 0.0)

    t_lane = jnp.where(lane < 64, lane - (NI - HEAD), lane - (LANES - 2 * SIX))
    t_lane = jnp.where(t_lane >= SIX, t_lane - SIX, t_lane)
    t_lane = NI * (64 + t_lane) + jnp.where(lane < 64, 0, NI - 1)
    second = ((lane < 64) & (lane >= NI - HEAD + SIX)) | (lane >= LANES - SIX)

    def put(ref, r, one, two):
        n2, s2 = roll(two[0], NI - NORTH), roll(two[1], NI)
        ref[r, 0] = jnp.where(lane < NI, roll(one[0], -NORTH), n2)
        ref[r, 1] = jnp.where(lane < NI, one[1], s2)
        ends = jnp.where(second, pick(two[3], t_lane), pick(one[3], t_lane))
        ref[r, 2] = jnp.where(
            lane < NI - HEAD, n2,
            jnp.where((lane >= 64) & (lane < LANES - 2 * SIX), roll(two[1], 64 - HEAD), ends),
        )
        ref[r, 3] = one[2]
        ref[r, 4] = two[2]

    def to_inner(r, src, gath, ssem, rsem):
        return [
            send(src, gath.at[member, pl.ds(0, src.shape[0])], ssem.at[r, o], rsem.at[r, o], in_inner(o, relay))
            for o in list(range(1, inner)) + [0]
        ]

    def send_m(r, gath, s_p, lm_p):
        t_p = [total(x * w) for x, w in zip(lm_p, wet_p)]
        p_p = [total(x * w) for x, w in zip(s_p, wet_p)]
        t_p[0], p_p[0] = roll(t_p[0], -NORTH), roll(p_p[0], -NORTH)
        out = t_p[0]
        for k, x in enumerate(t_p[1:] + p_p):
            out = jnp.where(sub == k + 1, x, out)
        m_s[r] = out
        gath[member] = out
        return [
            send(m_s.at[r], gath.at[member], m1_send.at[r, o], m1_recv.at[r, o], in_inner(o, d))
            for o in range(1, inner)
        ]

    def send_a(r, gath, m_p, s_p):
        put(a_s, r, [x * w for x, w in zip(m_p, wet_p)], [x * w for x, w in zip(s_p, wet_p)])
        if r == 0:
            out = roll(wet_p[0], -NORTH)
            for k in range(1, 4):
                out = jnp.where(sub == k, wet_p[k], out)
            a_s[r, 5] = out
        return to_inner(r, a_s.at[r] if r == 0 else a_s.at[r, pl.ds(0, 5)], gath, a1_send, a1_recv)

    def adjoint(lm_p, lt_p):
        wm = [a * b for a, b in zip(mdif_p, lm_p)]
        u = [a * b + press * running(c, False) for a, b, c in zip(tdif_p, lt_p, lm_p)]
        return wm, u

    def send_b(r, gath, wm, u):
        put(b_s, r, [x * w for x, w in zip(wm, wet_p)], [x * w for x, w in zip(u, wet_p)])
        return to_inner(r, b_s.at[r], gath, b1_send, b1_recv)

    gath_a, gath_b, gath_m = (ga_0, ga_1), (gb_0, gb_1), (gm_0, gm_1)

    pl.semaphore_wait(barrier, len(greeted))
    table_copies = [
        send(table, tables.at[o], tab_send.at[o], tab_recv.at[o], in_outer(o, relay))
        for o in list(range(1, outer)) + [0]
    ]
    adj = adjoint(state[2], state[3])
    first_m = send_m(0, gath_m[0], state[1], state[2])
    first_a = send_a(0, gath_a[0], state[0], state[1])
    first_b = send_b(0, gath_b[0], *adj)

    routes = {}

    def route(o):
        if o not in routes:
            slot = (outer - o) % outer
            found = []
            for k in range(4):
                tile = tables_s[slot, 0, k]
                edge = tables_s[slot, 1, k]
                known = jnp.maximum(tile, 0)
                here = (tile >= 0) & (lax.div(known, inner) == group)
                found.append((lax.rem(known, inner), edge, jnp.where(here, 1.0, 0.0)))
            routes[o] = found
        return routes[o]

    def either(x, turned, straight):
        return x * straight + turned * (1.0 - straight)

    def relayed(gath, o):
        (tn, en, hn), (ts, es, hs), (te, ee, he), (tw, ew, hw) = route(o)
        en, es = jnp.where(en == 0, 0, 1), jnp.where(es == 0, 0, 1)
        fn, fs = 1.0 - en.astype(f32), es.astype(f32)
        fe, fw = jnp.where(ee == 3, 1.0, 0.0), jnp.where(ew == 2, 1.0, 0.0)
        v_n = gath[tn, en] * hn
        v_s = gath[ts, es] * hs
        x_n, x_s, x_e, x_w = gath[tn, 2] * hn, gath[ts, 2] * hs, gath[te, 2] * he, gath[tw, 2] * hw
        x_n, x_s = either(x_n, roll(x_n, 64), fn), either(x_s, roll(x_s, 64), fs)
        x_e, x_w = either(x_e, roll(x_e, 64), fe), either(x_w, roll(x_w, 64), fw)
        v_r = jnp.where(
            lane < 64, jnp.where(lane < NI - HEAD, x_n, x_e), jnp.where(lane < LANES - 2 * SIX, x_s, x_w)
        )
        sides = []
        for k in (3, 4):
            e, w = gath[te, k] * he, gath[tw, k] * hw
            sides.append(jnp.where(odd, either(w, roll(w, NI - 1), fw), either(e, roll(e, 1 - NI), fe)))
        return [v_n, v_s, v_r] + sides

    def relayed_rows(load, o, at):
        (tn, en, hn), (ts, es, hs), (te, ee, he), (tw, ew, hw) = route(o)
        fn, fs = jnp.where(en == 0, 1.0, 0.0), jnp.where(es == 0, 0.0, 1.0)
        fe, fw = jnp.where(ee == 3, 1.0, 0.0), jnp.where(ew == 2, 1.0, 0.0)
        n, s, e, w = load(tn) * hn, load(ts) * hs, load(te) * he, load(tw) * hw
        n, s = either(n, roll(n, -1, 0), fn), either(s, roll(s, 1, 0), fs)
        e, w = either(e, roll(e, 1 - NI), fe), either(w, roll(w, NI - 1), fw)
        return jnp.where(at == 0, n, jnp.where(at == 1, s, jnp.where(odd, w, e)))

    far_first = sorted(range(outer), key=lambda o: -min(o, outer - o))

    def relay_a(r):
        copies = []
        for o in far_first:
            out = relayed(gath_a[r], o)
            if r == 0:
                out.append(relayed_rows(lambda t: gath_a[0][t, 5], o, sub))
            for k, x in enumerate(out):
                ha_s[r, o, k] = x
            span = pl.ds(0, len(out))
            copies.append(send(
                ha_s.at[r, o, span], ha_r.at[r, o, span], a2_send.at[r, o], a2_recv.at[r, o], in_outer(o, relay)
            ))
        return copies

    def relay_b(r):
        copies = []
        for o in far_first:
            for k, x in enumerate(relayed(gath_b[r], o)):
                hb_s[r, o, k] = x
            copies.append(send(hb_s.at[r, o], hb_r.at[r, o], b2_send.at[r, o], b2_recv.at[r, o], in_outer(o, relay)))
        return copies

    def relay_m(r):
        copies = []
        for o in far_first:
            hm_s[r, o] = relayed_rows(lambda t: gath_m[r][t], o, sub & 3)
            for k in range(1, depth):
                copies.append(send(
                    hm_s.at[r, o], hm_r.at[r, o, k], m2_send.at[r, o, k], m2_recv.at[r, o, k],
                    in_outer(o, shifted(k)),
                ))
        return copies

    def prepare(loads, lo, last):
        m, s, lm, lt = [load(lo, last) for load in loads]
        w = wet_at(lo, last)
        mixed = mix(lo, last) * lt
        back = running(lm, False)
        at = slice(LANES + MAIN, LANES + WIDTH) if last else pl.ds(pl.multiple_of(lo + LANES, LANES), BLOCK)
        grid[0:rows, at] = w * m
        grid[rows : 2 * rows, at] = w * s
        grid[3 * rows : 4 * rows, at] = w * (mdif(lo, last) * lm)
        grid[4 * rows : 5 * rows, at] = w * (tdif(lo, last) * lt + press * back)
        out = jnp.where(level == 0, s, total(s))
        out = jnp.where(level == 1, roll(mixed, 1, 0), out)
        out = jnp.where(level == 2, roll(back, 2, 0), out)
        out = jnp.where(level == 3, roll(s, 4, 0), out)
        out = jnp.where(level == 4, roll(mixed, 5, 0), out)
        return out

    def prepare_all(r, body):
        def step(b, carry):
            lo = pl.multiple_of(b * BLOCK, LANES)
            edge_s[r, :, pl.ds(lo, BLOCK)] = body(lo, False)
            return carry
        lax.fori_loop(0, BLOCKS, step, 0)
        edge_s[r, :, MAIN:WIDTH] = body(MAIN, True)
        return [
            send(edge_s.at[r], edge_r.at[r, o], e_send.at[r, o], e_recv.at[r, o], {"tiles": me, "depth": shifted(o)})
            for o in range(1, depth)
        ]

    def origin(o):
        return lax.rem(d + depth - o, depth)

    shallower = [None] + [jnp.where(origin(o) < d, 1.0, 0.0) for o in range(1, depth)]
    deeper = [None] + [jnp.where(origin(o) > d, 1.0, 0.0) for o in range(1, depth)]
    has_above = jnp.where(d > 0, 1.0, 0.0)
    has_below = jnp.where(d < depth - 1, 1.0, 0.0)

    def others(r, edges):
        def body(lo, last):
            w = wet_at(lo, last)
            out = jnp.where(level == 2, w, 0.0)
            for o in range(1, depth):
                x = edge_r[r, o, :, MAIN:WIDTH] if last else edge_r[r, o, :, pl.ds(lo, BLOCK)]
                x = x * w
                out = out + jnp.where(level == 0, roll(x, -5, 0) * shallower[o], 0.0)
                out = out + jnp.where(level == 1, roll(x, -1, 0) * (deeper[o] * press), 0.0)
            at = slice(LANES + MAIN, LANES + WIDTH) if last else pl.ds(pl.multiple_of(lo + LANES, LANES), BLOCK)
            grid[2 * rows : 3 * rows, at] = out

        def step(b, carry):
            body(pl.multiple_of(b * BLOCK, LANES), False)
            return carry

        if depth > 1:
            lax.fori_loop(0, BLOCKS, step, 0)
            body(MAIN, True)

    def advance(r, loads):
        def around(g, lo, last, e, w):
            span = slice(g * rows, (g + 1) * rows)
            x = grid[span, MAIN:GRID] if last else grid[span, pl.ds(lo, BLOCK + 2 * LANES)]
            def at(k):
                return roll(x, -k)[:, LANES : LANES + BLOCK]
            return at(NI) + at(-NI) + at(1) * e + at(-1) * w, x[:, LANES : LANES + BLOCK]

        def body(lo, last):
            e, w, wet = keep_e(lo, last), keep_w(lo, last), wet_at(lo, last)
            sums, own_x = around(2, lo, last, e, w)
            weights = sums[2:3]
            lap_x = wet * sums - weights * own_x
            def lap(g):
                sums, own = around(g, lo, last, e, w)
                return wet * sums - weights * own
            m, s, lm, lt = [load(lo, last) for load in loads]
            mx = mix(lo, last)
            mixed = mx * lt

            def vertical(q, which):
                above, below = q[0:1], q[rows - 1 : rows]
                if depth > 1:
                    x = edge_r[r, 1, :, MAIN:WIDTH] if last else edge_r[r, 1, :, pl.ds(lo, BLOCK)]
                    y = x if depth == 2 else (
                        edge_r[r, depth - 1, :, MAIN:WIDTH] if last else edge_r[r, depth - 1, :, pl.ds(lo, BLOCK)]
                    )
                    above = x[3 + which : 4 + which] * has_above + above * (1.0 - has_above)
                    below = y[which : which + 1] * has_below + below * (1.0 - has_below)
                up = jnp.where(level == 0, above, roll(q, 1, 0))
                down = jnp.where(level == rows - 1, below, roll(q, rows - 1, 0))
                return (up - q) + (down - q)

            lap_s = lap(1)
            results = [
                m + mdif(lo, last) * lap(0) + press * (running(lap_s, True) + lap_x[0:1]),
                s + tdif(lo, last) * lap_s + mx * vertical(s, 0) + 0.2 * m,
                lm + lap(3) + 0.2 * lt,
                lt + vertical(mixed, 1) + lap(4) + lap_x[1:2],
            ]
            for k, x in enumerate(results):
                if last:
                    base[k, :, MAIN:WIDTH] = x
                else:
                    base[k, :, pl.ds(lo, BLOCK)] = x
            return results + [own_x]

        norths, accs, tails = sweep(body, 5)
        souths = [base[k, :, 0:LANES] for k in range(4)] + [grid[2 * rows : 3 * rows, LANES : 2 * LANES]]
        return [list(p) for p in zip(norths, souths, accs, tails)]

    def merged(ref, r, k):
        out = ref[r, 0, k]
        for o in range(1, outer):
            out = out + ref[r, o, k]
        return out

    def opened(ref, r):
        v_n, v_s, v_r, e_1, e_2 = [merged(ref, r, k) for k in range(5)]
        one = [pick(v_n, i_n), pick(v_s, i_s)]
        two = [
            jnp.where(i_n < HEAD, pick(v_n, NI + i_n), pick(v_r, i_n - HEAD)),
            jnp.where(i_s < HEAD, pick(v_s, NI + i_s), pick(v_r, 64 + i_s - HEAD)),
        ]
        for k, (out, e) in enumerate(((one, e_1), (two, e_2))):
            out.append(jnp.where(m_main, pick(e, m_from), pick(v_r, m_rest + SIX * k)))
            out.append(jnp.where(t_main, pick(e, t_from), pick(v_r, t_rest + SIX * k)))
        return one, two

    def opened_rows(x):
        ew, tl = pick(x, m_from), pick(x, t_from)
        return [pick(x, i_n), pick(x, i_s), ew, tl]

    def opened_wet():
        n, s, ew, tl = opened_rows(merged(ha_r, 0, 5))
        return [
            jnp.broadcast_to(n[0:1], n.shape), jnp.broadcast_to(s[1:2], s.shape),
            jnp.where(m_main, ew[2:3], ew[3:4]), jnp.where(t_main, tl[2:3], tl[3:4]),
        ]

    def opened_m(r):
        x = None
        for k in range(1, depth):
            y = None
            for o in range(outer):
                y = hm_r[r, o, k] if y is None else y + hm_r[r, o, k]
            y = y * jnp.where(sub < 4, deeper[k] * press, shallower[k])
            x = y if x is None else x + y
        if x is None:
            return [jnp.zeros((rows, LANES), f32)] * 4
        n, s, ew, tl = opened_rows(x)

        def rows_of(p, t):
            return jnp.where(sub == 0, p, jnp.where(sub == 1, t, 0.0))

        return [
            rows_of(n[4:5], n[0:1]), rows_of(s[5:6], s[1:2]),
            rows_of(jnp.where(m_main, ew[6:7], ew[7:8]), jnp.where(m_main, ew[2:3], ew[3:4])),
            rows_of(jnp.where(t_main, tl[6:7], tl[7:8]), jnp.where(t_main, tl[2:3], tl[3:4])),
        ]

    def gained(halo, own, wet_h):
        return [w * (h - v * q) for w, h, v, q in zip(wet_p, halo, wet_h, own)]

    def spread(old, gain):
        n, s, ew, tl = gain
        return [
            old[0] + n + jnp.where(corner_n, tl, 0.0),
            old[1] + s + jnp.where(corner_s, ew, 0.0),
            old[2] + ew + jnp.where(corner_s, s, 0.0),
            old[3] + tl + jnp.where(corner_n, n, 0.0),
        ]

    def add_ends(gains):
        for k in range(4):
            base[k, :, 0:LANES] = base[k, :, 0:LANES] + gains[k][1]
            at = slice(MAIN + 3 * LANES, MAIN + 4 * LANES)
            base[k, :, at] = base[k, :, at] + jnp.where(lane >= NORTH, gains[k][0], 0.0)
            at = slice(MAIN + 4 * LANES, WIDTH)
            base[k, :, at] = base[k, :, at] + jnp.where(lane < NORTH + NI - LANES, gains[k][0], 0.0)

    def filled(k, gains, lo, last):
        side = jnp.concatenate([gains[k][3 if last else 2]] * (BLOCK // LANES), axis=1)
        return kept(k)(lo, last) + on(lo, last) * side

    loads = [field(r) for r in (mom_ref, tra_ref, mcot_ref, tcot_ref)]
    wet_h = gains = None
    for r in range(2):
        if r == 0:
            edges = prepare_all(r, functools.partial(prepare, loads))
        else:
            add_ends(gains)

            def body(lo, last):
                values = [filled(k, gains, lo, last) for k in range(4)]
                for k, x in enumerate(values):
                    if last:
                        base[k, :, MAIN:WIDTH] = x
                    else:
                        base[k, :, pl.ds(lo, BLOCK)] = x
                return prepare([lambda lo, last, x=x: x for x in values], lo, last)

            edges = prepare_all(r, body)
            loads = [kept(k) for k in range(4)]

        if r == 0:
            for copy in table_copies:
                copy.wait_recv()
            local = pltpu.make_async_copy(tables, tables_s, tab_local)
            local.start()
            local.wait()
        for copy in first_a:
            copy.wait_recv()
        second_a = relay_a(r)
        if r == 0:
            for copy in first_m:
                copy.wait_recv()
            second_m = relay_m(r)
        for copy in first_b:
            copy.wait_recv()
        second_b = relay_b(r)
        if r == 1:
            for copy in first_m:
                copy.wait_recv()
            second_m = relay_m(r)

        for copy in edges:
            copy.wait_recv()
        others(r, edges)
        bases = advance(r, loads)
        wm, u = adj

        for copy in second_a:
            copy.wait_recv()
        for copy in second_m:
            copy.wait_recv()
        if r == 0:
            wet_h = opened_wet()
        h_m, h_s = opened(ha_r, r)
        g_x = gained(opened_m(r), bases[4], wet_h)
        g_m, g_s = gained(h_m, state[0], wet_h), gained(h_s, state[1], wet_h)
        gain_m = [c * a + press * (running(b, True) + x[0:1]) for c, a, b, x in zip(mdif_p, g_m, g_s, g_x)]
        gain_s = [c * a for c, a in zip(tdif_p, g_s)]
        if r == 0:
            m_p, s_p = spread(bases[0], gain_m), spread(bases[1], gain_s)
            first_a = send_a(1, gath_a[1], m_p, s_p)
        for copy in second_b:
            copy.wait_recv()
        h_w, h_u = opened(hb_r, r)
        gain_lm = gained(h_w, wm, wet_h)
        gain_lt = [a + x[1:2] for a, x in zip(gained(h_u, u, wet_h), g_x)]
        if r == 0:
            lm_p, lt_p = spread(bases[2], gain_lm), spread(bases[3], gain_lt)
            adj = adjoint(lm_p, lt_p)
            first_b = send_b(1, gath_b[1], *adj)
            first_m = send_m(1, gath_m[1], s_p, lm_p)
            state = [m_p, s_p, lm_p, lt_p]
        gains = [gain_m, gain_s, gain_lm, gain_lt]

    add_ends(gains)
    outs = (mom_out, tra_out, mgrad_out, tgrad_out)

    def finish(b, carry):
        lo = pl.multiple_of(b * BLOCK, LANES)
        for k, out in enumerate(outs):
            out[0, :, pl.ds(lo, BLOCK)] = filled(k, gains, lo, False)
        return carry

    lax.fori_loop(0, BLOCKS, finish, 0)
    for k, out in enumerate(outs):
        out[0, :, MAIN:CELLS] = filled(k, gains, MAIN, True)[:, :REST]
    for copy in started:
        copy.wait_send()


def write_out(*refs):
    sources, targets, staged, sems = refs[:4], refs[4:8], refs[8:12], refs[12]
    reads = [pltpu.make_async_copy(sources[k], staged[k], sems.at[0, k]) for k in range(4)]
    writes = [pltpu.make_async_copy(staged[k], targets[k], sems.at[1, k]) for k in range(4)]
    for copy in reads:
        copy.start()
    for read, write in zip(reads, writes):
        read.wait()
        write.start()
    for copy in writes:
        copy.wait()


def solution(mesh):
    tiles, depth = mesh.shape["tiles"], mesh.shape["depth"]
    inner = max(k for k in range(1, tiles + 1) if tiles % k == 0 and k * k <= tiles)
    outer = tiles // inner

    def local(*args):
        rows = args[0].shape[1]
        dma = pltpu.SemaphoreType.DMA
        f32 = jnp.float32
        shape = jax.ShapeDtypeStruct(args[0].shape, f32)
        vmem = pl.BlockSpec(memory_space=pltpu.VMEM)
        hbm = pl.BlockSpec(memory_space=pltpu.MemorySpace.HBM)

        def strips(*lead):
            return pltpu.VMEM((*lead, rows, LANES), f32)

        results = pl.pallas_call(
            functools.partial(kernel, inner, outer, depth, rows * depth),
            out_shape=(shape,) * 4,
            in_specs=[hbm] * 11,
            out_specs=(vmem,) * 4,
            scratch_shapes=[
                *[pltpu.VMEM(a.shape, a.dtype) for a in args],
                pltpu.SMEM((1, 4), jnp.int32),
                *[pltpu.VMEM((rows, WIDTH), f32)] * 4,
                pltpu.VMEM((5 * rows, GRID), f32),
                pltpu.VMEM((4, rows, WIDTH), f32),
                pltpu.VMEM((2, rows, WIDTH), f32),
                pltpu.VMEM((2, depth, rows, WIDTH), f32),
                strips(2, 6), strips(2, 5), strips(2),
                strips(inner, 6), strips(inner, 6), strips(inner, 5), strips(inner, 5), strips(inner), strips(inner),
                strips(2, outer, 6), strips(2, outer, 5), strips(2, outer),
                strips(2, outer, 6), strips(2, outer, 5), strips(2, outer, depth),
                pltpu.VMEM((8, LANES), jnp.int32),
                pltpu.VMEM((outer, 8, LANES), jnp.int32),
                pltpu.SMEM((outer, 8, LANES), jnp.int32),
                dma((10,)), dma(()), dma((outer,)), dma((outer,)), dma(()), dma((2, depth)), dma((2, depth)),
                *[dma((2, inner))] * 6,
                *[dma((2, outer))] * 4, *[dma((2, outer, depth))] * 2,
            ],
            compiler_params=pltpu.CompilerParams(
                collective_id=0, has_side_effects=True, vmem_limit_bytes=62 * 1024 * 1024
            ),
        )(*args)
        return pl.pallas_call(
            write_out,
            out_shape=(shape,) * 4,
            in_specs=[pl.BlockSpec(memory_space=pl.ANY)] * 4,
            out_specs=(hbm,) * 4,
            scratch_shapes=[pltpu.VMEM(shape.shape, f32)] * 4 + [dma((2, 4))],
            compiler_params=pltpu.CompilerParams(vmem_limit_bytes=62 * 1024 * 1024),
        )(*results)

    whole = P("tiles", "depth", None)
    flat = P("tiles", None)
    in_specs = (whole,) * 5 + (flat,) * 4 + (whole,) * 2
    return jax.shard_map(local, mesh=mesh, in_specs=in_specs, out_specs=(whole,) * 4, check_vma=False)
```

```python
import functools

import jax
import jax.numpy as jnp
from jax import lax
from jax.experimental import pallas as pl
from jax.experimental.pallas import tpu as pltpu
from jax.sharding import PartitionSpec as P

NI = 90
NJ = 70
CELLS = NI * NJ
LANES = 128
MAIN = 64 * NI
BLOCK = 5 * LANES
BLOCKS = MAIN // BLOCK
WIDTH = MAIN + BLOCK
REST = CELLS - MAIN
GRID = WIDTH + 2 * LANES
NORTH = NI * (NJ - 1) % LANES
HEAD = LANES - NI
SIX = NJ - 64
INVERSE = 37
MESH = pl.DeviceIdType.MESH


def roll(x, shift, axis=1):
    return pltpu.roll(x, shift % x.shape[axis], axis)


def pick(x, lanes):
    return jnp.take_along_axis(x, lanes & (LANES - 1), axis=1, mode="promise_in_bounds")


def kernel(
    inner, outer, depth, levels_all,
    mom_hbm, tra_hbm, mdif_hbm, tdif_hbm, mix_hbm, wet_hbm, nb_hbm, se_hbm, fl_hbm, mcot_hbm, tcot_hbm,
    mom_out, tra_out, mgrad_out, tgrad_out,
    mom_ref, tra_ref, mdif_ref, tdif_ref, mix_ref, wet_ref, nb_ref, se_ref, fl_ref, mcot_ref, tcot_ref,
    fl_s, on_ref, ke_ref, kw_ref, wet8, grid, base, edge_s, edge_r,
    a_s, b_s, m_s, ga_0, ga_1, gb_0, gb_1, gm_0, gm_1, ha_s, hb_s, hm_s, ha_r, hb_r, hm_r,
    table, tables, tables_s,
    in_sem, fl_sem, tab_send, tab_recv, tab_local, e_send, e_recv,
    a1_send, a1_recv, b1_send, b1_recv, m1_send, m1_recv,
    a2_send, a2_recv, b2_send, b2_recv, m2_send, m2_recv,
):
    me = lax.axis_index("tiles")
    d = lax.axis_index("depth")
    member = lax.rem(me, inner)
    group = lax.div(me, inner)
    relay = depth - 1 - d
    rows = mom_ref.shape[1]
    press = -0.1 * levels_all ** (-0.5)
    f32 = jnp.float32

    def in_inner(o, at):
        return {"tiles": group * inner + lax.rem(member + o, inner), "depth": at}

    def in_outer(o, at):
        return {"tiles": lax.rem(group + o, outer) * inner + member, "depth": at}

    def shifted(o):
        return lax.rem(d + o, depth)

    small = pltpu.make_async_copy(fl_hbm, fl_s, fl_sem)
    small.start()
    fetched = []
    for k, (src, dst) in enumerate((
        (nb_hbm, nb_ref), (se_hbm, se_ref), (wet_hbm, wet_ref), (mom_hbm, mom_ref), (tra_hbm, tra_ref),
        (mcot_hbm, mcot_ref), (tcot_hbm, tcot_ref), (mdif_hbm, mdif_ref), (tdif_hbm, tdif_ref), (mix_hbm, mix_ref),
    )):
        fetched.append(pltpu.make_async_copy(src, dst, in_sem.at[k]))
        fetched[-1].start()
    barrier = pltpu.get_barrier_semaphore()
    greeted = [in_inner(o, at) for o in range(1, inner) for at in (d, relay)]
    greeted += [in_outer(o, shifted(k)) for o in range(outer) for k in range(1, depth)]
    for device in greeted:
        pl.semaphore_signal(barrier, inc=1, device_id=device, device_id_type=MESH)

    started = []
    far_first = sorted(range(outer), key=lambda o: -min(o, outer - o))

    def send(src, dst, ssem, rsem, to):
        copy = pltpu.make_async_remote_copy(
            src_ref=src, dst_ref=dst, send_sem=ssem, recv_sem=rsem, device_id=to, device_id_type=MESH
        )
        copy.start()
        started.append(copy)
        return copy

    lane = lax.broadcasted_iota(jnp.int32, (rows, LANES), 1)
    sub = lax.broadcasted_iota(jnp.int32, (rows, LANES), 0)
    level = lax.broadcasted_iota(jnp.int32, (rows, BLOCK), 0)
    place = lax.broadcasted_iota(jnp.int32, (rows, BLOCK), 1).astype(f32)
    odd = (lane & 1) == 1
    i_n = (lane + LANES - NORTH) & (LANES - 1)
    i_s = lane
    j_m = (jnp.where(odd, (lane + LANES - NI + 1) >> 1, lane >> 1) * INVERSE) & 63
    j_t = jnp.full_like(lane, -1)
    for j in range(64, NJ):
        for x in (NI * j % LANES, (NI * j + NI - 1) % LANES):
            j_t = jnp.where(lane == x, j, j_t)
    is_t = j_t >= 0
    corner_s = (lane == 0) | (lane == NI - 1)
    corner_n = (lane == NORTH) | (lane == (NORTH + NI - 1) % LANES)

    zero = jnp.zeros((5 * rows, LANES), f32)
    grid[:, 0:LANES] = zero
    grid[:, GRID - 2 * LANES : GRID - LANES] = zero
    grid[:, GRID - LANES :] = zero
    table[...] = jnp.zeros_like(table)

    def marks(b, carry):
        lo = pl.multiple_of(b * BLOCK, LANES)
        pos = place + lo.astype(f32)
        col = pos - NI * jnp.floor((pos + 0.5) * (1.0 / NI))
        inside = pos < CELLS - 0.5
        west = (col < 0.5) & inside
        east = (col > NI - 1.5) & inside
        on_ref[:, pl.ds(lo, BLOCK)] = jnp.where(west | east, 1.0, 0.0)
        ke_ref[:, pl.ds(lo, BLOCK)] = jnp.where(east, 0.0, 1.0)
        kw_ref[:, pl.ds(lo, BLOCK)] = jnp.where(west, 0.0, 1.0)
        return carry

    lax.fori_loop(0, BLOCKS + 1, marks, 0)

    small.wait()
    for copy in fetched[:2]:
        copy.wait()
    table[0:1, 0:4] = nb_ref[...]
    table[1:2, 0:4] = se_ref[...]
    pl.semaphore_wait(barrier, len(greeted))
    table_copies = [
        send(table, tables.at[k], tab_send.at[k], tab_recv.at[k], to)
        for k, to in [(o, in_outer(o, relay)) for o in list(range(1, outer)) + [0]]
        + [(outer + o - 1, in_inner(o, relay)) for o in range(1, inner)]
    ]
    flip = [fl_s[0, k] for k in range(4)]
    f_ew = jnp.where(odd, flip[2], flip[3])
    i_n = i_n + flip[0] * (NI - 1 - 2 * i_n)
    i_s = i_s + flip[1] * (NI - 1 - 2 * i_s)
    j_m = j_m + f_ew * (NJ - 1 - 2 * j_m)
    j_t = j_t + f_ew * (NJ - 1 - 2 * j_t)
    m_main, t_main = j_m < 64, j_t < 64
    shift = jnp.where(odd, 0, NI - 1)
    m_from, t_from = NI * j_m + shift, NI * j_t + shift
    shift = jnp.where(odd, NI - HEAD, LANES - 2 * SIX) - 64
    m_rest, t_rest = j_m + shift, j_t + shift

    for copy in fetched[2:]:
        copy.wait()

    def padded(x):
        return jnp.concatenate([x, jnp.zeros((x.shape[0], BLOCK - REST), x.dtype)], axis=1)

    def field(ref):
        def load(lo, last):
            return padded(ref[0, :, MAIN:CELLS]) if last else ref[0, :, pl.ds(lo, BLOCK)]
        return load

    def kept(k):
        def load(lo, last):
            return base[k, :, MAIN:WIDTH] if last else base[k, :, pl.ds(lo, BLOCK)]
        return load

    def wide(ref):
        def load(lo, last):
            return ref[:, MAIN:WIDTH] if last else ref[:, pl.ds(lo, BLOCK)]
        return load

    def wet_int(lo, last):
        x = padded(wet_ref[0:1, MAIN:CELLS]) if last else wet_ref[0:1, pl.ds(lo, BLOCK)]
        return jnp.broadcast_to(x.astype(f32), (rows, BLOCK))

    mdif, tdif, mix = field(mdif_ref), field(tdif_ref), field(mix_ref)
    on, keep_e, keep_w, wet_at = wide(on_ref), wide(ke_ref), wide(kw_ref), wide(wet8)

    def cut(x, c):
        return x[:, c * LANES : (c + 1) * LANES]

    def collect(acc, x, mask):
        for c in range(BLOCK // LANES):
            acc = jnp.where(cut(mask, c) > 0.5, cut(x, c), acc)
        return acc

    def sweep(body, count):
        def step(b, accs):
            lo = pl.multiple_of(b * BLOCK, LANES)
            mask = on(lo, False)
            return tuple(collect(a, x, mask) for a, x in zip(accs, body(lo, False)))
        accs = lax.fori_loop(0, BLOCKS, step, (jnp.zeros((rows, LANES), f32),) * count)
        mask = on(MAIN, True)
        ends = body(MAIN, True)
        tails = [collect(jnp.zeros((rows, LANES), f32), x, mask) for x in ends]
        norths = [jnp.where(lane >= NORTH, cut(x, 3), cut(x, 4)) for x in ends]
        return norths, accs, tails

    def running(x, down):
        at = lax.broadcasted_iota(jnp.int32, x.shape, 0)
        k = 1
        while k < rows:
            if down:
                x = x + jnp.where(at >= k, roll(x, k, 0), 0.0)
            else:
                x = x + jnp.where(at < rows - k, roll(x, rows - k, 0), 0.0)
            k *= 2
        return x

    def total(x):
        k = rows // 2
        while k >= 1:
            x = x + roll(x, k, 0)
            k //= 2
        return x

    sources = [field(r) for r in (mom_ref, tra_ref, mcot_ref, tcot_ref, mdif_ref, tdif_ref)]

    def first_body(lo, last):
        w = wet_int(lo, last)
        if last:
            wet8[:, MAIN:WIDTH] = w
        else:
            wet8[:, pl.ds(lo, BLOCK)] = w
        return [load(lo, last) for load in sources] + [w]

    norths, accs, tails = sweep(first_body, 7)
    souths = [r[0, :, 0:LANES] for r in (mom_ref, tra_ref, mcot_ref, tcot_ref, mdif_ref, tdif_ref)] + [wet8[:, 0:LANES]]
    packs = [list(p) for p in zip(norths, souths, accs, tails)]
    state = packs[:4]
    mdif_p, tdif_p, wet_p = packs[4:]
    wet_p[0] = jnp.where((lane >= NORTH) | (lane < NORTH + NI - LANES), wet_p[0], 0.0)
    wet_p[1] = jnp.where(lane < NI, wet_p[1], 0.0)
    wet_p[3] = jnp.where(is_t, wet_p[3], 0.0)

    t_lane = jnp.where(lane < 64, lane - (NI - HEAD), lane - (LANES - 2 * SIX))
    t_lane = jnp.where(t_lane >= SIX, t_lane - SIX, t_lane)
    t_lane = NI * (64 + t_lane) + jnp.where(lane < 64, 0, NI - 1)
    second = ((lane < 64) & (lane >= NI - HEAD + SIX)) | (lane >= LANES - SIX)

    def put(ref, r, one, two):
        n2, s2 = roll(two[0], NI - NORTH), roll(two[1], NI)
        ref[r, 0] = jnp.where(lane < NI, roll(one[0], -NORTH), n2)
        ref[r, 1] = jnp.where(lane < NI, one[1], s2)
        ends = jnp.where(second, pick(two[3], t_lane), pick(one[3], t_lane))
        ref[r, 2] = jnp.where(
            lane < NI - HEAD, n2,
            jnp.where((lane >= 64) & (lane < LANES - 2 * SIX), roll(two[1], 64 - HEAD), ends),
        )
        ref[r, 3] = one[2]
        ref[r, 4] = two[2]

    def to_inner(r, src, gath, ssem, rsem):
        return [
            send(src, gath.at[member, pl.ds(0, src.shape[0])], ssem.at[r, o], rsem.at[r, o], in_inner(o, relay))
            for o in list(range(1, inner)) + [0]
        ]

    def send_m(r, gath, s_p, lm_p):
        t_p = [total(x * w) for x, w in zip(lm_p, wet_p)]
        p_p = [total(x * w) for x, w in zip(s_p, wet_p)]
        t_p[0], p_p[0] = roll(t_p[0], -NORTH), roll(p_p[0], -NORTH)
        out = t_p[0]
        for k, x in enumerate(t_p[1:] + p_p):
            out = jnp.where(sub == k + 1, x, out)
        m_s[r] = out
        gath[member] = out
        return [
            send(m_s.at[r], gath.at[member], m1_send.at[r, o], m1_recv.at[r, o], in_inner(o, d))
            for o in range(1, inner)
        ]

    def send_a(r, gath, m_p, s_p):
        put(a_s, r, [x * w for x, w in zip(m_p, wet_p)], [x * w for x, w in zip(s_p, wet_p)])
        if r == 0:
            out = roll(wet_p[0], -NORTH)
            for k in range(1, 4):
                out = jnp.where(sub == k, wet_p[k], out)
            a_s[r, 5] = out
        return to_inner(r, a_s.at[r] if r == 0 else a_s.at[r, pl.ds(0, 5)], gath, a1_send, a1_recv)

    def adjoint(lm_p, lt_p):
        wm = [a * b for a, b in zip(mdif_p, lm_p)]
        u = [a * b + press * running(c, False) for a, b, c in zip(tdif_p, lt_p, lm_p)]
        return wm, u

    def send_b(r, gath, wm, u):
        put(b_s, r, [x * w for x, w in zip(wm, wet_p)], [x * w for x, w in zip(u, wet_p)])
        return [
            send(b_s.at[r], gath.at[group], b1_send.at[r, o], b1_recv.at[r, o], in_outer(o, relay)) for o in far_first
        ]

    gath_a, gath_b, gath_m = (ga_0, ga_1), (gb_0, gb_1), (gm_0, gm_1)

    adj = adjoint(state[2], state[3])
    first_m = send_m(0, gath_m[0], state[1], state[2])
    first_a = send_a(0, gath_a[0], state[0], state[1])
    first_b = send_b(0, gath_b[0], *adj)

    routes = {}

    def route(o, across):
        if (o, across) not in routes:
            if across:
                slot = outer + inner - o - 1 if o else 0
            else:
                slot = (outer - o) % outer
            found = []
            for k in range(4):
                tile = tables_s[slot, 0, k]
                edge = tables_s[slot, 1, k]
                known = jnp.maximum(tile, 0)
                its_group, its_member = lax.div(known, inner), lax.rem(known, inner)
                if across:
                    here, spot = its_member == member, its_group
                else:
                    here, spot = its_group == group, its_member
                found.append((spot, edge, jnp.where((tile >= 0) & here, 1.0, 0.0)))
            routes[o, across] = found
        return routes[o, across]

    def either(x, turned, straight):
        return x * straight + turned * (1.0 - straight)

    def relayed(gath, o, across):
        (tn, en, hn), (ts, es, hs), (te, ee, he), (tw, ew, hw) = route(o, across)
        en, es = jnp.where(en == 0, 0, 1), jnp.where(es == 0, 0, 1)
        fn, fs = 1.0 - en.astype(f32), es.astype(f32)
        fe, fw = jnp.where(ee == 3, 1.0, 0.0), jnp.where(ew == 2, 1.0, 0.0)
        v_n = gath[tn, en] * hn
        v_s = gath[ts, es] * hs
        x_n, x_s, x_e, x_w = gath[tn, 2] * hn, gath[ts, 2] * hs, gath[te, 2] * he, gath[tw, 2] * hw
        x_n, x_s = either(x_n, roll(x_n, 64), fn), either(x_s, roll(x_s, 64), fs)
        x_e, x_w = either(x_e, roll(x_e, 64), fe), either(x_w, roll(x_w, 64), fw)
        v_r = jnp.where(
            lane < 64, jnp.where(lane < NI - HEAD, x_n, x_e), jnp.where(lane < LANES - 2 * SIX, x_s, x_w)
        )
        sides = []
        for k in (3, 4):
            e, w = gath[te, k] * he, gath[tw, k] * hw
            sides.append(jnp.where(odd, either(w, roll(w, NI - 1), fw), either(e, roll(e, 1 - NI), fe)))
        return [v_n, v_s, v_r] + sides

    def relayed_rows(load, o, at):
        (tn, en, hn), (ts, es, hs), (te, ee, he), (tw, ew, hw) = route(o, False)
        fn, fs = jnp.where(en == 0, 1.0, 0.0), jnp.where(es == 0, 0.0, 1.0)
        fe, fw = jnp.where(ee == 3, 1.0, 0.0), jnp.where(ew == 2, 1.0, 0.0)
        n, s, e, w = load(tn) * hn, load(ts) * hs, load(te) * he, load(tw) * hw
        n, s = either(n, roll(n, -1, 0), fn), either(s, roll(s, 1, 0), fs)
        e, w = either(e, roll(e, 1 - NI), fe), either(w, roll(w, NI - 1), fw)
        return jnp.where(at == 0, n, jnp.where(at == 1, s, jnp.where(odd, w, e)))

    def relay_a(r):
        copies = []
        for o in far_first:
            out = relayed(gath_a[r], o, False)
            if r == 0:
                out.append(relayed_rows(lambda t: gath_a[0][t, 5], o, sub))
            for k, x in enumerate(out):
                ha_s[r, o, k] = x
            span = pl.ds(0, len(out))
            copies.append(send(
                ha_s.at[r, o, span], ha_r.at[r, o, span], a2_send.at[r, o], a2_recv.at[r, o], in_outer(o, relay)
            ))
        return copies

    def relay_b(r):
        copies = []
        for o in list(range(1, inner)) + [0]:
            for k, x in enumerate(relayed(gath_b[r], o, True)):
                hb_s[r, o, k] = x
            copies.append(send(hb_s.at[r, o], hb_r.at[r, o], b2_send.at[r, o], b2_recv.at[r, o], in_inner(o, relay)))
        return copies

    def relay_m(r):
        copies = []
        for o in far_first:
            hm_s[r, o] = relayed_rows(lambda t: gath_m[r][t], o, sub & 3)
            for k in range(1, depth):
                copies.append(send(
                    hm_s.at[r, o], hm_r.at[r, o, k], m2_send.at[r, o, k], m2_recv.at[r, o, k],
                    in_outer(o, shifted(k)),
                ))
        return copies

    def prepare(loads, lo, last):
        m, s, lm, lt = [load(lo, last) for load in loads]
        w = wet_at(lo, last)
        mixed = mix(lo, last) * lt
        back = running(lm, False)
        at = slice(LANES + MAIN, LANES + WIDTH) if last else pl.ds(pl.multiple_of(lo + LANES, LANES), BLOCK)
        grid[0:rows, at] = w * m
        grid[rows : 2 * rows, at] = w * s
        grid[3 * rows : 4 * rows, at] = w * (mdif(lo, last) * lm)
        grid[4 * rows : 5 * rows, at] = w * (tdif(lo, last) * lt + press * back)
        out = jnp.where(level == 0, s, total(s))
        out = jnp.where(level == 1, roll(mixed, 1, 0), out)
        out = jnp.where(level == 2, roll(back, 2, 0), out)
        out = jnp.where(level == 3, roll(s, 4, 0), out)
        out = jnp.where(level == 4, roll(mixed, 5, 0), out)
        return out

    def prepare_all(r, body):
        def step(b, carry):
            lo = pl.multiple_of(b * BLOCK, LANES)
            edge_s[r, :, pl.ds(lo, BLOCK)] = body(lo, False)
            return carry
        lax.fori_loop(0, BLOCKS, step, 0)
        edge_s[r, :, MAIN:WIDTH] = body(MAIN, True)
        return [
            send(edge_s.at[r], edge_r.at[r, o], e_send.at[r, o], e_recv.at[r, o], {"tiles": me, "depth": shifted(o)})
            for o in range(1, depth)
        ]

    def origin(o):
        return lax.rem(d + depth - o, depth)

    shallower = [None] + [jnp.where(origin(o) < d, 1.0, 0.0) for o in range(1, depth)]
    deeper = [None] + [jnp.where(origin(o) > d, 1.0, 0.0) for o in range(1, depth)]
    has_above = jnp.where(d > 0, 1.0, 0.0)
    has_below = jnp.where(d < depth - 1, 1.0, 0.0)

    def others(r, edges):
        def body(lo, last):
            w = wet_at(lo, last)
            out = jnp.where(level == 2, w, 0.0)
            for o in range(1, depth):
                x = edge_r[r, o, :, MAIN:WIDTH] if last else edge_r[r, o, :, pl.ds(lo, BLOCK)]
                x = x * w
                out = out + jnp.where(level == 0, roll(x, -5, 0) * shallower[o], 0.0)
                out = out + jnp.where(level == 1, roll(x, -1, 0) * (deeper[o] * press), 0.0)
            at = slice(LANES + MAIN, LANES + WIDTH) if last else pl.ds(pl.multiple_of(lo + LANES, LANES), BLOCK)
            grid[2 * rows : 3 * rows, at] = out

        def step(b, carry):
            body(pl.multiple_of(b * BLOCK, LANES), False)
            return carry

        if depth > 1:
            lax.fori_loop(0, BLOCKS, step, 0)
            body(MAIN, True)

    def advance(r, loads):
        def around(g, lo, last, e, w):
            span = slice(g * rows, (g + 1) * rows)
            x = grid[span, MAIN:GRID] if last else grid[span, pl.ds(lo, BLOCK + 2 * LANES)]
            def at(k):
                return roll(x, -k)[:, LANES : LANES + BLOCK]
            return at(NI) + at(-NI) + at(1) * e + at(-1) * w, x[:, LANES : LANES + BLOCK]

        def body(lo, last):
            e, w, wet = keep_e(lo, last), keep_w(lo, last), wet_at(lo, last)
            sums, own_x = around(2, lo, last, e, w)
            weights = sums[2:3]
            lap_x = wet * sums - weights * own_x
            def lap(g):
                sums, own = around(g, lo, last, e, w)
                return wet * sums - weights * own
            m, s, lm, lt = [load(lo, last) for load in loads]
            mx = mix(lo, last)
            mixed = mx * lt

            def vertical(q, which):
                above, below = q[0:1], q[rows - 1 : rows]
                if depth > 1:
                    x = edge_r[r, 1, :, MAIN:WIDTH] if last else edge_r[r, 1, :, pl.ds(lo, BLOCK)]
                    y = x if depth == 2 else (
                        edge_r[r, depth - 1, :, MAIN:WIDTH] if last else edge_r[r, depth - 1, :, pl.ds(lo, BLOCK)]
                    )
                    above = x[3 + which : 4 + which] * has_above + above * (1.0 - has_above)
                    below = y[which : which + 1] * has_below + below * (1.0 - has_below)
                up = jnp.where(level == 0, above, roll(q, 1, 0))
                down = jnp.where(level == rows - 1, below, roll(q, rows - 1, 0))
                return (up - q) + (down - q)

            lap_s = lap(1)
            results = [
                m + mdif(lo, last) * lap(0) + press * (running(lap_s, True) + lap_x[0:1]),
                s + tdif(lo, last) * lap_s + mx * vertical(s, 0) + 0.2 * m,
                lm + lap(3) + 0.2 * lt,
                lt + vertical(mixed, 1) + lap(4) + lap_x[1:2],
            ]
            for k, x in enumerate(results):
                if last:
                    base[k, :, MAIN:WIDTH] = x
                else:
                    base[k, :, pl.ds(lo, BLOCK)] = x
            return results + [own_x]

        norths, accs, tails = sweep(body, 5)
        souths = [base[k, :, 0:LANES] for k in range(4)] + [grid[2 * rows : 3 * rows, LANES : 2 * LANES]]
        return [list(p) for p in zip(norths, souths, accs, tails)]

    def merged(ref, r, k):
        out = ref[r, 0, k]
        for o in range(1, ref.shape[1]):
            out = out + ref[r, o, k]
        return out

    def opened(ref, r):
        v_n, v_s, v_r, e_1, e_2 = [merged(ref, r, k) for k in range(5)]
        one = [pick(v_n, i_n), pick(v_s, i_s)]
        two = [
            jnp.where(i_n < HEAD, pick(v_n, NI + i_n), pick(v_r, i_n - HEAD)),
            jnp.where(i_s < HEAD, pick(v_s, NI + i_s), pick(v_r, 64 + i_s - HEAD)),
        ]
        for k, (out, e) in enumerate(((one, e_1), (two, e_2))):
            out.append(jnp.where(m_main, pick(e, m_from), pick(v_r, m_rest + SIX * k)))
            out.append(jnp.where(t_main, pick(e, t_from), pick(v_r, t_rest + SIX * k)))
        return one, two

    def opened_rows(x):
        ew, tl = pick(x, m_from), pick(x, t_from)
        return [pick(x, i_n), pick(x, i_s), ew, tl]

    def opened_wet():
        n, s, ew, tl = opened_rows(merged(ha_r, 0, 5))
        return [
            jnp.broadcast_to(n[0:1], n.shape), jnp.broadcast_to(s[1:2], s.shape),
            jnp.where(m_main, ew[2:3], ew[3:4]), jnp.where(t_main, tl[2:3], tl[3:4]),
        ]

    def opened_m(r):
        x = None
        for k in range(1, depth):
            y = None
            for o in range(outer):
                y = hm_r[r, o, k] if y is None else y + hm_r[r, o, k]
            y = y * jnp.where(sub < 4, deeper[k] * press, shallower[k])
            x = y if x is None else x + y
        if x is None:
            return [jnp.zeros((rows, LANES), f32)] * 4
        n, s, ew, tl = opened_rows(x)

        def rows_of(p, t):
            return jnp.where(sub == 0, p, jnp.where(sub == 1, t, 0.0))

        return [
            rows_of(n[4:5], n[0:1]), rows_of(s[5:6], s[1:2]),
            rows_of(jnp.where(m_main, ew[6:7], ew[7:8]), jnp.where(m_main, ew[2:3], ew[3:4])),
            rows_of(jnp.where(t_main, tl[6:7], tl[7:8]), jnp.where(t_main, tl[2:3], tl[3:4])),
        ]

    def gained(halo, own, wet_h):
        return [w * (h - v * q) for w, h, v, q in zip(wet_p, halo, wet_h, own)]

    def spread(old, gain):
        n, s, ew, tl = gain
        return [
            old[0] + n + jnp.where(corner_n, tl, 0.0),
            old[1] + s + jnp.where(corner_s, ew, 0.0),
            old[2] + ew + jnp.where(corner_s, s, 0.0),
            old[3] + tl + jnp.where(corner_n, n, 0.0),
        ]

    def add_ends(gains):
        for k in range(4):
            base[k, :, 0:LANES] = base[k, :, 0:LANES] + gains[k][1]
            at = slice(MAIN + 3 * LANES, MAIN + 4 * LANES)
            base[k, :, at] = base[k, :, at] + jnp.where(lane >= NORTH, gains[k][0], 0.0)
            at = slice(MAIN + 4 * LANES, WIDTH)
            base[k, :, at] = base[k, :, at] + jnp.where(lane < NORTH + NI - LANES, gains[k][0], 0.0)

    def filled(k, gains, lo, last):
        side = jnp.concatenate([gains[k][3 if last else 2]] * (BLOCK // LANES), axis=1)
        return kept(k)(lo, last) + on(lo, last) * side

    loads = [field(r) for r in (mom_ref, tra_ref, mcot_ref, tcot_ref)]
    wet_h = gains = None
    for r in range(2):
        if r == 0:
            edges = prepare_all(r, functools.partial(prepare, loads))
        else:
            add_ends(gains)

            def body(lo, last):
                values = [filled(k, gains, lo, last) for k in range(4)]
                for k, x in enumerate(values):
                    if last:
                        base[k, :, MAIN:WIDTH] = x
                    else:
                        base[k, :, pl.ds(lo, BLOCK)] = x
                return prepare([lambda lo, last, x=x: x for x in values], lo, last)

            edges = prepare_all(r, body)
            loads = [kept(k) for k in range(4)]

        if r == 0:
            for copy in table_copies:
                copy.wait_recv()
            local = pltpu.make_async_copy(tables, tables_s, tab_local)
            local.start()
            local.wait()
        for copy in first_a:
            copy.wait_recv()
        second_a = relay_a(r)
        if r == 0:
            for copy in first_m:
                copy.wait_recv()
            second_m = relay_m(r)
        for copy in first_b:
            copy.wait_recv()
        second_b = relay_b(r)
        if r == 1:
            for copy in first_m:
                copy.wait_recv()
            second_m = relay_m(r)

        for copy in edges:
            copy.wait_recv()
        others(r, edges)
        bases = advance(r, loads)
        wm, u = adj

        for copy in second_a:
            copy.wait_recv()
        for copy in second_m:
            copy.wait_recv()
        if r == 0:
            wet_h = opened_wet()
        h_m, h_s = opened(ha_r, r)
        g_x = gained(opened_m(r), bases[4], wet_h)
        g_m, g_s = gained(h_m, state[0], wet_h), gained(h_s, state[1], wet_h)
        gain_m = [c * a + press * (running(b, True) + x[0:1]) for c, a, b, x in zip(mdif_p, g_m, g_s, g_x)]
        gain_s = [c * a for c, a in zip(tdif_p, g_s)]
        if r == 0:
            m_p, s_p = spread(bases[0], gain_m), spread(bases[1], gain_s)
            first_a = send_a(1, gath_a[1], m_p, s_p)
        for copy in second_b:
            copy.wait_recv()
        h_w, h_u = opened(hb_r, r)
        gain_lm = gained(h_w, wm, wet_h)
        gain_lt = [a + x[1:2] for a, x in zip(gained(h_u, u, wet_h), g_x)]
        if r == 0:
            lm_p, lt_p = spread(bases[2], gain_lm), spread(bases[3], gain_lt)
            adj = adjoint(lm_p, lt_p)
            first_b = send_b(1, gath_b[1], *adj)
            first_m = send_m(1, gath_m[1], s_p, lm_p)
            state = [m_p, s_p, lm_p, lt_p]
        gains = [gain_m, gain_s, gain_lm, gain_lt]

    add_ends(gains)
    outs = (mom_out, tra_out, mgrad_out, tgrad_out)

    def finish(b, carry):
        lo = pl.multiple_of(b * BLOCK, LANES)
        for k, out in enumerate(outs):
            out[0, :, pl.ds(lo, BLOCK)] = filled(k, gains, lo, False)
        return carry

    lax.fori_loop(0, BLOCKS, finish, 0)
    for k, out in enumerate(outs):
        out[0, :, MAIN:CELLS] = filled(k, gains, MAIN, True)[:, :REST]
    for copy in started:
        copy.wait_send()


def write_out(*refs):
    sources, targets, sems = refs[:4], refs[4:8], refs[8]
    writes = [pltpu.make_async_copy(sources[k], targets[k], sems.at[k]) for k in range(4)]
    for copy in writes:
        copy.start()
    for copy in writes:
        copy.wait()


def solution(mesh):
    tiles, depth = mesh.shape["tiles"], mesh.shape["depth"]
    inner = max(k for k in range(1, tiles + 1) if tiles % k == 0 and k * k <= tiles)
    outer = tiles // inner

    def local(*args):
        rows = args[0].shape[1]
        dma = pltpu.SemaphoreType.DMA
        f32 = jnp.float32
        shape = jax.ShapeDtypeStruct(args[0].shape, f32)
        vmem = pl.BlockSpec(memory_space=pltpu.VMEM)
        hbm = pl.BlockSpec(memory_space=pltpu.MemorySpace.HBM)

        def strips(*lead):
            return pltpu.VMEM((*lead, rows, LANES), f32)

        results = pl.pallas_call(
            functools.partial(kernel, inner, outer, depth, rows * depth),
            out_shape=(pltpu.VMEM(shape.shape, f32),) * 4,
            in_specs=[hbm] * 11,
            out_specs=(vmem,) * 4,
            scratch_shapes=[
                *[pltpu.VMEM(a.shape, a.dtype) for a in args],
                pltpu.SMEM((1, 4), jnp.int32),
                *[pltpu.VMEM((rows, WIDTH), f32)] * 4,
                pltpu.VMEM((5 * rows, GRID), f32),
                pltpu.VMEM((4, rows, WIDTH), f32),
                pltpu.VMEM((2, rows, WIDTH), f32),
                pltpu.VMEM((2, depth, rows, WIDTH), f32),
                strips(2, 6), strips(2, 5), strips(2),
                strips(inner, 6), strips(inner, 6), strips(outer, 5), strips(outer, 5), strips(inner), strips(inner),
                strips(2, outer, 6), strips(2, inner, 5), strips(2, outer),
                strips(2, outer, 6), strips(2, inner, 5), strips(2, outer, depth),
                pltpu.VMEM((8, LANES), jnp.int32),
                pltpu.VMEM((outer + inner - 1, 8, LANES), jnp.int32),
                pltpu.SMEM((outer + inner - 1, 8, LANES), jnp.int32),
                dma((10,)), dma(()), dma((outer + inner - 1,)), dma((outer + inner - 1,)), dma(()), dma((2, depth)), dma((2, depth)),
                *[dma((2, inner))] * 2, *[dma((2, outer))] * 2, *[dma((2, inner))] * 2,
                *[dma((2, outer))] * 2, *[dma((2, inner))] * 2, *[dma((2, outer, depth))] * 2,
            ],
            compiler_params=pltpu.CompilerParams(
                collective_id=0, has_side_effects=True, vmem_limit_bytes=62 * 1024 * 1024
            ),
        )(*args)
        return pl.pallas_call(
            write_out,
            out_shape=(shape,) * 4,
            in_specs=[vmem] * 4,
            out_specs=(hbm,) * 4,
            scratch_shapes=[dma((4,))],
            compiler_params=pltpu.CompilerParams(vmem_limit_bytes=62 * 1024 * 1024),
        )(*[pltpu.with_memory_space_constraint(x, pltpu.VMEM) for x in results])

    whole = P("tiles", "depth", None)
    flat = P("tiles", None)
    in_specs = (whole,) * 5 + (flat,) * 4 + (whole,) * 2
    return jax.shard_map(local, mesh=mesh, in_specs=in_specs, out_specs=(whole,) * 4, check_vma=False)
```

```python
import functools

import jax
import jax.numpy as jnp
from jax import lax
from jax.experimental import pallas as pl
from jax.experimental.pallas import tpu as pltpu
from jax.sharding import PartitionSpec as P

NI = 90
NJ = 70
CELLS = NI * NJ
LANES = 128
MAIN = 64 * NI
BLOCK = 5 * LANES
BLOCKS = MAIN // BLOCK
WIDTH = MAIN + BLOCK
REST = CELLS - MAIN
GRID = WIDTH + 2 * LANES
NORTH = NI * (NJ - 1) % LANES
HEAD = LANES - NI
SIX = NJ - 64
INVERSE = 37
MESH = pl.DeviceIdType.MESH


def roll(x, shift, axis=1):
    return pltpu.roll(x, shift % x.shape[axis], axis)


def pick(x, lanes):
    return jnp.take_along_axis(x, lanes & (LANES - 1), axis=1, mode="promise_in_bounds")


def kernel(
    inner, outer, depth, levels_all,
    mom_hbm, tra_hbm, mdif_hbm, tdif_hbm, mix_hbm, wet_hbm, nb_hbm, se_hbm, fl_hbm, mcot_hbm, tcot_hbm,
    mom_out, tra_out, mgrad_out, tgrad_out,
    fields, wet_ref, nb_ref, se_ref, fl_s, on_ref, ke_ref, kw_ref, wet8, grid, base, edge_s, edge_r,
    a_s, b_s, p_s, t_s, ga_0, ga_1, gb_0, gb_1, gp_0, gp_1, gt_0, gt_1, ha_s, hb_s, ha_r, hb_r, hp_r, ht_r,
    table, tables,
    bulk, in_sem, send_sem, tab_recv, e_recv, a1_recv, b1_recv, a2_recv, b2_recv, p2_recv, t2_recv,
):
    me = lax.axis_index("tiles")
    d = lax.axis_index("depth")
    member = lax.rem(me, inner)
    group = lax.div(me, inner)
    relay = depth - 1 - d
    rows = fields.shape[1]
    press = -0.1 * levels_all ** (-0.5)
    f32 = jnp.float32

    def in_inner(o, at):
        return {"tiles": group * inner + lax.rem(member + o, inner), "depth": at}

    def in_outer(o, at):
        return {"tiles": lax.rem(group + o, outer) * inner + member, "depth": at}

    def shifted(o):
        return lax.rem(d + o, depth)

    fetched = [pltpu.make_async_copy(nb_hbm, nb_ref, in_sem.at[0]), pltpu.make_async_copy(se_hbm, se_ref, in_sem.at[1])]
    fetched.append(pltpu.make_async_copy(fl_hbm, fl_s, in_sem.at[2]))
    fetched.append(pltpu.make_async_copy(wet_hbm, wet_ref, in_sem.at[3]))
    parts = ((0, 2), (2, 6), (6, 7))
    for k, src in enumerate((mom_hbm, tra_hbm, mcot_hbm, mdif_hbm, tcot_hbm, tdif_hbm, mix_hbm)):
        group_of = [n for n, (a, b) in enumerate(parts) if a <= k < b][0]
        fetched.append(pltpu.make_async_copy(src, fields.at[pl.ds(k, 1)], in_sem.at[4 + group_of]))
    for copy in fetched:
        copy.start()

    def fields_in(n):
        part = fields.at[pl.ds(parts[n][0], parts[n][1] - parts[n][0])]
        pltpu.make_async_copy(part, part, in_sem.at[4 + n]).wait()

    barrier = pltpu.get_barrier_semaphore()
    greeted = [in_inner(o, at) for o in range(1, inner) for at in (d, relay)]
    greeted += [in_outer(o, shifted(k)) for o in range(outer) for k in range(depth) if o or k]
    for device in greeted:
        pl.semaphore_signal(barrier, inc=1, device_id=device, device_id_type=MESH)

    sent = [0]

    def size(ref):
        count = 1
        for n in ref.shape:
            count *= n
        return count // LANES

    def send(src, dst, rsem, to):
        pltpu.make_async_remote_copy(
            src_ref=src, dst_ref=dst, send_sem=send_sem, recv_sem=rsem, device_id=to, device_id_type=MESH
        ).start()
        sent[0] += size(dst)
        assert sent[0] <= bulk.shape[0]
        return size(dst)

    def arrived(count, sem):
        part = bulk.at[pl.ds(0, count)]
        pltpu.make_async_copy(part, part, sem).wait()

    far_first = sorted(range(outer), key=lambda o: -min(o, outer - o))

    lane = lax.broadcasted_iota(jnp.int32, (rows, LANES), 1)
    sub = lax.broadcasted_iota(jnp.int32, (rows, LANES), 0)
    level = lax.broadcasted_iota(jnp.int32, (rows, BLOCK), 0)
    place = lax.broadcasted_iota(jnp.int32, (rows, BLOCK), 1).astype(f32)
    odd = (lane & 1) == 1
    i_n = (lane + LANES - NORTH) & (LANES - 1)
    i_s = lane
    j_m = (jnp.where(odd, (lane + LANES - NI + 1) >> 1, lane >> 1) * INVERSE) & 63
    j_t = jnp.full_like(lane, -1)
    for j in range(64, NJ):
        for x in (NI * j % LANES, (NI * j + NI - 1) % LANES):
            j_t = jnp.where(lane == x, j, j_t)
    is_t = j_t >= 0
    corner_s = (lane == 0) | (lane == NI - 1)
    corner_n = (lane == NORTH) | (lane == (NORTH + NI - 1) % LANES)

    zero = jnp.zeros((5 * rows, LANES), f32)
    grid[:, 0:LANES] = zero
    grid[:, GRID - 2 * LANES : GRID - LANES] = zero
    grid[:, GRID - LANES :] = zero
    table[...] = jnp.zeros_like(table)

    def marks(b, carry):
        lo = pl.multiple_of(b * BLOCK, LANES)
        pos = place + lo.astype(f32)
        col = pos - NI * jnp.floor((pos + 0.5) * (1.0 / NI))
        inside = pos < CELLS - 0.5
        west = (col < 0.5) & inside
        east = (col > NI - 1.5) & inside
        on_ref[:, pl.ds(lo, BLOCK)] = jnp.where(west | east, 1.0, 0.0)
        ke_ref[:, pl.ds(lo, BLOCK)] = jnp.where(east, 0.0, 1.0)
        kw_ref[:, pl.ds(lo, BLOCK)] = jnp.where(west, 0.0, 1.0)
        return carry

    lax.fori_loop(0, BLOCKS + 1, marks, 0)

    for copy in fetched[:3]:
        copy.wait()
    table[:, 0:4] = nb_ref[...]
    table[:, 4:8] = se_ref[...]
    pl.semaphore_wait(barrier, len(greeted))
    table_rows = sum(
        send(table, tables.at[k], tab_recv, to)
        for k, to in [(o, in_outer(o, relay)) for o in list(range(1, outer)) + [0]]
        + [(outer + o - 1, in_inner(o, relay)) for o in range(1, inner)]
    )
    flip = [fl_s[0, k] for k in range(4)]
    f_ew = jnp.where(odd, flip[2], flip[3])
    i_n = i_n + flip[0] * (NI - 1 - 2 * i_n)
    i_s = i_s + flip[1] * (NI - 1 - 2 * i_s)
    j_m = j_m + f_ew * (NJ - 1 - 2 * j_m)
    j_t = j_t + f_ew * (NJ - 1 - 2 * j_t)
    m_main, t_main = j_m < 64, j_t < 64
    shift = jnp.where(odd, 0, NI - 1)
    m_from, t_from = NI * j_m + shift, NI * j_t + shift
    shift = jnp.where(odd, NI - HEAD, LANES - 2 * SIX) - 64
    m_rest, t_rest = j_m + shift, j_t + shift

    def padded(x):
        return jnp.concatenate([x, jnp.zeros((x.shape[0], BLOCK - REST), x.dtype)], axis=1)

    def field(k):
        def load(lo, last):
            return padded(fields[k, :, MAIN:CELLS]) if last else fields[k, :, pl.ds(lo, BLOCK)]
        return load

    def kept(k):
        def load(lo, last):
            return base[k, :, MAIN:WIDTH] if last else base[k, :, pl.ds(lo, BLOCK)]
        return load

    def wide(ref):
        def load(lo, last):
            return ref[:, MAIN:WIDTH] if last else ref[:, pl.ds(lo, BLOCK)]
        return load

    def wet_int(lo, last):
        x = padded(wet_ref[0:1, MAIN:CELLS]) if last else wet_ref[0:1, pl.ds(lo, BLOCK)]
        return jnp.broadcast_to(x.astype(f32), (rows, BLOCK))

    mdif, tdif, mix = field(3), field(5), field(6)
    on, keep_e, keep_w, wet_at = wide(on_ref), wide(ke_ref), wide(kw_ref), wide(wet8)

    def cut(x, c):
        return x[:, c * LANES : (c + 1) * LANES]

    def collect(acc, x, mask):
        for c in range(BLOCK // LANES):
            acc = jnp.where(cut(mask, c) > 0.5, cut(x, c), acc)
        return acc

    def sweep(body, count):
        def step(b, accs):
            lo = pl.multiple_of(b * BLOCK, LANES)
            mask = on(lo, False)
            return tuple(collect(a, x, mask) for a, x in zip(accs, body(lo, False)))
        accs = lax.fori_loop(0, BLOCKS, step, (jnp.zeros((rows, LANES), f32),) * count)
        mask = on(MAIN, True)
        ends = body(MAIN, True)
        tails = [collect(jnp.zeros((rows, LANES), f32), x, mask) for x in ends]
        norths = [jnp.where(lane >= NORTH, cut(x, 3), cut(x, 4)) for x in ends]
        return norths, accs, tails

    def running(x, down):
        at = lax.broadcasted_iota(jnp.int32, x.shape, 0)
        k = 1
        while k < rows:
            if down:
                x = x + jnp.where(at >= k, roll(x, k, 0), 0.0)
            else:
                x = x + jnp.where(at < rows - k, roll(x, rows - k, 0), 0.0)
            k *= 2
        return x

    def total(x):
        k = rows // 2
        while k >= 1:
            x = x + roll(x, k, 0)
            k //= 2
        return x

    def packed(refs, masked):
        sources = [field(r) for r in refs]

        def body(lo, last):
            values = [load(lo, last) for load in sources]
            if masked:
                values.append(wet_int(lo, last))
                if last:
                    wet8[:, MAIN:WIDTH] = values[-1]
                else:
                    wet8[:, pl.ds(lo, BLOCK)] = values[-1]
            return values

        norths, accs, tails = sweep(body, len(refs) + masked)
        souths = [fields[k, :, 0:LANES] for k in refs] + [wet8[:, 0:LANES]] * masked
        return [list(p) for p in zip(norths, souths, accs, tails)]

    fetched[3].wait()
    fields_in(0)
    m_p, s_p, wet_p = packed([0, 1], 1)
    wet_p[0] = jnp.where((lane >= NORTH) | (lane < NORTH + NI - LANES), wet_p[0], 0.0)
    wet_p[1] = jnp.where(lane < NI, wet_p[1], 0.0)
    wet_p[3] = jnp.where(is_t, wet_p[3], 0.0)

    t_lane = jnp.where(lane < 64, lane - (NI - HEAD), lane - (LANES - 2 * SIX))
    t_lane = jnp.where(t_lane >= SIX, t_lane - SIX, t_lane)
    t_lane = NI * (64 + t_lane) + jnp.where(lane < 64, 0, NI - 1)
    second = ((lane < 64) & (lane >= NI - HEAD + SIX)) | (lane >= LANES - SIX)

    def put(ref, r, one, two):
        n2, s2 = roll(two[0], NI - NORTH), roll(two[1], NI)
        ref[r, 0] = jnp.where(lane < NI, roll(one[0], -NORTH), n2)
        ref[r, 1] = jnp.where(lane < NI, one[1], s2)
        ends = jnp.where(second, pick(two[3], t_lane), pick(one[3], t_lane))
        ref[r, 2] = jnp.where(
            lane < NI - HEAD, n2,
            jnp.where((lane >= 64) & (lane < LANES - 2 * SIX), roll(two[1], 64 - HEAD), ends),
        )
        ref[r, 3] = one[2]
        ref[r, 4] = two[2]

    def sums(packs):
        n, s, ew, tl = [total(x * w) for x, w in zip(packs, wet_p)]
        n = roll(n, -NORTH)
        out = jnp.where(sub == 0, n, jnp.where(sub == 1, s, jnp.where(sub == 2, ew, tl)))
        return out[0:4]

    def send_p(r, gath, s_p):
        p_s[r] = gath[member] = sums(s_p)
        return sum(send(p_s.at[r], gath.at[member], a1_recv.at[r], in_inner(o, d)) for o in range(1, inner))

    def send_t(r, gath, lm_p):
        t_s[r] = gath[group] = sums(lm_p)
        return sum(send(t_s.at[r], gath.at[group], b1_recv.at[r], in_outer(o, d)) for o in far_first if o)

    def send_a(r, gath, m_p, s_p):
        put(a_s, r, [x * w for x, w in zip(m_p, wet_p)], [x * w for x, w in zip(s_p, wet_p)])
        if r == 0:
            out = jnp.where(sub == 4, roll(wet_p[0], -NORTH), 0.0)
            for k in range(1, 4):
                out = jnp.where(sub == 4 + k, wet_p[k], out)
            a_s[r, 5] = out
        span = pl.ds(0, 6 - r)
        return sum(
            send(a_s.at[r, span], gath.at[member, span], a1_recv.at[r], in_inner(o, relay))
            for o in list(range(1, inner)) + [0]
        )

    def adjoint(mdif_p, tdif_p, lm_p, lt_p):
        wm = [a * b for a, b in zip(mdif_p, lm_p)]
        u = [a * b + press * running(c, False) for a, b, c in zip(tdif_p, lt_p, lm_p)]
        return wm, u

    def send_b(r, gath, wm, u):
        put(b_s, r, [x * w for x, w in zip(wm, wet_p)], [x * w for x, w in zip(u, wet_p)])
        return sum(send(b_s.at[r], gath.at[group], b1_recv.at[r], in_outer(o, relay)) for o in far_first)

    gath_a, gath_b, gath_p, gath_t = (ga_0, ga_1), (gb_0, gb_1), (gp_0, gp_1), (gt_0, gt_1)

    first_a = send_p(0, gath_p[0], s_p)
    first_a += send_a(0, gath_a[0], m_p, s_p)
    fields_in(1)
    lm_p, mdif_p, lt_p, tdif_p = packed([2, 3, 4, 5], 0)
    state = [m_p, s_p, lm_p, lt_p]
    first_b = send_t(0, gath_t[0], lm_p)
    adj = adjoint(mdif_p, tdif_p, lm_p, lt_p)
    first_b += send_b(0, gath_b[0], *adj)
    fields_in(2)

    routes = {}

    def route(o, across):
        if (o, across) not in routes:
            if across:
                slot = outer + inner - o - 1 if o else 0
            else:
                slot = (outer - o) % outer
            found = []
            for k in range(4):
                tile = tables[slot, 0, k]
                edge = tables[slot, 0, 4 + k]
                known = jnp.maximum(tile, 0)
                its_group, its_member = lax.div(known, inner), lax.rem(known, inner)
                if across:
                    here, spot = its_member == member, its_group
                else:
                    here, spot = its_group == group, its_member
                found.append((spot, edge, jnp.where((tile >= 0) & here, 1.0, 0.0)))
            routes[o, across] = found
        return routes[o, across]

    def either(x, turned, straight):
        return x * straight + turned * (1.0 - straight)

    def relayed(gath, o, across):
        (tn, en, hn), (ts, es, hs), (te, ee, he), (tw, ew, hw) = route(o, across)
        en, es = jnp.where(en == 0, 0, 1), jnp.where(es == 0, 0, 1)
        fn, fs = 1.0 - en.astype(f32), es.astype(f32)
        fe, fw = jnp.where(ee == 3, 1.0, 0.0), jnp.where(ew == 2, 1.0, 0.0)
        v_n = gath[tn, en] * hn
        v_s = gath[ts, es] * hs
        x_n, x_s, x_e, x_w = gath[tn, 2] * hn, gath[ts, 2] * hs, gath[te, 2] * he, gath[tw, 2] * hw
        x_n, x_s = either(x_n, roll(x_n, 64), fn), either(x_s, roll(x_s, 64), fs)
        x_e, x_w = either(x_e, roll(x_e, 64), fe), either(x_w, roll(x_w, 64), fw)
        v_r = jnp.where(
            lane < 64, jnp.where(lane < NI - HEAD, x_n, x_e), jnp.where(lane < LANES - 2 * SIX, x_s, x_w)
        )
        sides = []
        for k in (3, 4):
            e, w = gath[te, k] * he, gath[tw, k] * hw
            sides.append(jnp.where(odd, either(w, roll(w, NI - 1), fw), either(e, roll(e, 1 - NI), fe)))
        return [v_n, v_s, v_r] + sides

    def relayed_rows(load, o, across):
        (tn, en, hn), (ts, es, hs), (te, ee, he), (tw, ew, hw) = route(o, across)
        at = sub & 3
        fn, fs = jnp.where(en == 0, 1.0, 0.0), jnp.where(es == 0, 0.0, 1.0)
        fe, fw = jnp.where(ee == 3, 1.0, 0.0), jnp.where(ew == 2, 1.0, 0.0)
        n, s, e, w = load(tn) * hn, load(ts) * hs, load(te) * he, load(tw) * hw
        n, s = either(n, roll(n, -1, 0), fn), either(s, roll(s, 1, 0), fs)
        e, w = either(e, roll(e, 1 - NI), fe), either(w, roll(w, NI - 1), fw)
        return jnp.where(at == 0, n, jnp.where(at == 1, s, jnp.where(odd, w, e)))

    def rows_at(ref, t):
        x = ref[t]
        return jnp.concatenate([x, x], axis=0)

    def to_depths(src, dst, r, o, rsem, place):
        return sum(send(src, dst.at[r, o, k], rsem.at[r], place(o, shifted(k))) for k in range(1, depth) if depth > 2)

    def relay_a(r):
        for o in far_first:
            out = relayed(gath_a[r], o, False)
            if r == 0:
                load = lambda t: jnp.where(sub < 4, rows_at(gath_p[0], t), gath_a[0][t, 5])
            else:
                load = lambda t: rows_at(gath_p[1], t)
            out.append(relayed_rows(load, o, False))
            for k, x in enumerate(out):
                ha_s[r, o, k] = x
        count = extra = 0
        for o in far_first:
            count += send(ha_s.at[r, o], ha_r.at[r, o], a2_recv.at[r], in_outer(o, relay))
            extra += to_depths(ha_s.at[r, o, 5], hp_r, r, o, p2_recv, in_outer)
        return count, extra

    def relay_b(r):
        spots = list(range(1, inner)) + [0]
        for o in spots:
            out = relayed(gath_b[r], o, True)
            out.append(relayed_rows(lambda t: rows_at(gath_t[r], t), o, True))
            for k, x in enumerate(out):
                hb_s[r, o, k] = x
        count = extra = 0
        for o in spots:
            count += send(hb_s.at[r, o], hb_r.at[r, o], b2_recv.at[r], in_inner(o, relay))
            extra += to_depths(hb_s.at[r, o, 5], ht_r, r, o, t2_recv, in_inner)
        return count, extra

    def prepare(loads, lo, last):
        m, s, lm, lt = [load(lo, last) for load in loads]
        w = wet_at(lo, last)
        mixed = mix(lo, last) * lt
        back = running(lm, False)
        at = slice(LANES + MAIN, LANES + WIDTH) if last else pl.ds(pl.multiple_of(lo + LANES, LANES), BLOCK)
        grid[0:rows, at] = w * m
        grid[rows : 2 * rows, at] = w * s
        grid[3 * rows : 4 * rows, at] = w * (mdif(lo, last) * lm)
        grid[4 * rows : 5 * rows, at] = w * (tdif(lo, last) * lt + press * back)
        out = jnp.where(level == 0, s, total(s))
        out = jnp.where(level == 1, roll(mixed, 1, 0), out)
        out = jnp.where(level == 2, roll(back, 2, 0), out)
        out = jnp.where(level == 3, roll(s, 4, 0), out)
        out = jnp.where(level == 4, roll(mixed, 5, 0), out)
        return out

    def prepare_all(r, body):
        def step(b, carry):
            lo = pl.multiple_of(b * BLOCK, LANES)
            edge_s[r, :, pl.ds(lo, BLOCK)] = body(lo, False)
            return carry
        lax.fori_loop(0, BLOCKS, step, 0)
        edge_s[r, :, MAIN:WIDTH] = body(MAIN, True)
        return sum(
            send(edge_s.at[r], edge_r.at[r, o], e_recv.at[r], {"tiles": me, "depth": shifted(o)})
            for o in range(1, depth)
        )

    def origin(o):
        return lax.rem(d + depth - o, depth)

    shallower = [None] + [jnp.where(origin(o) < d, 1.0, 0.0) for o in range(1, depth)]
    deeper = [None] + [jnp.where(origin(o) > d, 1.0, 0.0) for o in range(1, depth)]
    has_above = jnp.where(d > 0, 1.0, 0.0)
    has_below = jnp.where(d < depth - 1, 1.0, 0.0)

    def others(r, edges):
        def body(lo, last):
            w = wet_at(lo, last)
            out = jnp.where(level == 2, w, 0.0)
            for o in range(1, depth):
                x = edge_r[r, o, :, MAIN:WIDTH] if last else edge_r[r, o, :, pl.ds(lo, BLOCK)]
                x = x * w
                out = out + jnp.where(level == 0, roll(x, -5, 0) * shallower[o], 0.0)
                out = out + jnp.where(level == 1, roll(x, -1, 0) * deeper[o], 0.0)
            at = slice(LANES + MAIN, LANES + WIDTH) if last else pl.ds(pl.multiple_of(lo + LANES, LANES), BLOCK)
            grid[2 * rows : 3 * rows, at] = out

        def step(b, carry):
            body(pl.multiple_of(b * BLOCK, LANES), False)
            return carry

        if depth > 1:
            lax.fori_loop(0, BLOCKS, step, 0)
            body(MAIN, True)

    def advance(r, loads):
        def around(g, lo, last, e, w):
            span = slice(g * rows, (g + 1) * rows)
            x = grid[span, MAIN:GRID] if last else grid[span, pl.ds(lo, BLOCK + 2 * LANES)]
            def at(k):
                return roll(x, -k)[:, LANES : LANES + BLOCK]
            return at(NI) + at(-NI) + at(1) * e + at(-1) * w, x[:, LANES : LANES + BLOCK]

        def body(lo, last):
            e, w, wet = keep_e(lo, last), keep_w(lo, last), wet_at(lo, last)
            sums, own_x = around(2, lo, last, e, w)
            weights = sums[2:3]
            lap_x = wet * sums - weights * own_x
            def lap(g):
                sums, own = around(g, lo, last, e, w)
                return wet * sums - weights * own
            m, s, lm, lt = [load(lo, last) for load in loads]
            mx = mix(lo, last)
            mixed = mx * lt

            def vertical(q, which):
                above, below = q[0:1], q[rows - 1 : rows]
                if depth > 1:
                    x = edge_r[r, 1, :, MAIN:WIDTH] if last else edge_r[r, 1, :, pl.ds(lo, BLOCK)]
                    y = x if depth == 2 else (
                        edge_r[r, depth - 1, :, MAIN:WIDTH] if last else edge_r[r, depth - 1, :, pl.ds(lo, BLOCK)]
                    )
                    above = x[3 + which : 4 + which] * has_above + above * (1.0 - has_above)
                    below = y[which : which + 1] * has_below + below * (1.0 - has_below)
                up = jnp.where(level == 0, above, roll(q, 1, 0))
                down = jnp.where(level == rows - 1, below, roll(q, rows - 1, 0))
                return (up - q) + (down - q)

            lap_s = lap(1)
            results = [
                m + mdif(lo, last) * lap(0) + press * (running(lap_s, True) + lap_x[0:1]),
                s + tdif(lo, last) * lap_s + mx * vertical(s, 0) + 0.2 * m,
                lm + lap(3) + 0.2 * lt,
                lt + vertical(mixed, 1) + lap(4) + press * lap_x[1:2],
            ]
            for k, x in enumerate(results):
                if last:
                    base[k, :, MAIN:WIDTH] = x
                else:
                    base[k, :, pl.ds(lo, BLOCK)] = x
            return results + [own_x]

        norths, accs, tails = sweep(body, 5)
        souths = [base[k, :, 0:LANES] for k in range(4)] + [grid[2 * rows : 3 * rows, LANES : 2 * LANES]]
        return [list(p) for p in zip(norths, souths, accs, tails)]

    def merged(ref, r, k):
        out = ref[r, 0, k]
        for o in range(1, ref.shape[1]):
            out = out + ref[r, o, k]
        return out

    def opened(ref, r):
        v_n, v_s, v_r, e_1, e_2 = [merged(ref, r, k) for k in range(5)]
        one = [pick(v_n, i_n), pick(v_s, i_s)]
        two = [
            jnp.where(i_n < HEAD, pick(v_n, NI + i_n), pick(v_r, i_n - HEAD)),
            jnp.where(i_s < HEAD, pick(v_s, NI + i_s), pick(v_r, 64 + i_s - HEAD)),
        ]
        for k, (out, e) in enumerate(((one, e_1), (two, e_2))):
            out.append(jnp.where(m_main, pick(e, m_from), pick(v_r, m_rest + SIX * k)))
            out.append(jnp.where(t_main, pick(e, t_from), pick(v_r, t_rest + SIX * k)))
        return one, two

    def opened_rows(x, k):
        ew, tl = pick(x, m_from), pick(x, t_from)
        rows_of = [
            pick(x, i_n)[k : k + 1], pick(x, i_s)[k + 1 : k + 2],
            jnp.where(m_main, ew[k + 2 : k + 3], ew[k + 3 : k + 4]),
            jnp.where(t_main, tl[k + 2 : k + 3], tl[k + 3 : k + 4]),
        ]
        return [jnp.broadcast_to(y, (rows, LANES)) for y in rows_of]

    def opened_sums(attached, apart, r, gates):
        if depth == 2:
            x = merged(attached, r, 5) * gates[1]
        else:
            x = jnp.zeros((rows, LANES), f32)
            for k in range(1, depth):
                for o in range(apart.shape[1]):
                    x = x + apart[r, o, k] * gates[k]
        return opened_rows(x, 0)

    def gained(halo, own, wet_h):
        return [w * (h - v * q) for w, h, v, q in zip(wet_p, halo, wet_h, own)]

    def spread(old, gain):
        n, s, ew, tl = gain
        return [
            old[0] + n + jnp.where(corner_n, tl, 0.0),
            old[1] + s + jnp.where(corner_s, ew, 0.0),
            old[2] + ew + jnp.where(corner_s, s, 0.0),
            old[3] + tl + jnp.where(corner_n, n, 0.0),
        ]

    def add_ends(gains):
        for k in range(4):
            base[k, :, 0:LANES] = base[k, :, 0:LANES] + gains[k][1]
            at = slice(MAIN + 3 * LANES, MAIN + 4 * LANES)
            base[k, :, at] = base[k, :, at] + jnp.where(lane >= NORTH, gains[k][0], 0.0)
            at = slice(MAIN + 4 * LANES, WIDTH)
            base[k, :, at] = base[k, :, at] + jnp.where(lane < NORTH + NI - LANES, gains[k][0], 0.0)

    def filled(k, gains, lo, last):
        side = jnp.concatenate([gains[k][3 if last else 2]] * (BLOCK // LANES), axis=1)
        return kept(k)(lo, last) + on(lo, last) * side

    loads = [field(k) for k in (0, 1, 2, 4)]
    wet_h = gains = None
    for r in range(2):
        if r == 0:
            edges = prepare_all(r, functools.partial(prepare, loads))
        else:
            add_ends(gains)

            def body(lo, last):
                values = [filled(k, gains, lo, last) for k in range(4)]
                for k, x in enumerate(values):
                    if last:
                        base[k, :, MAIN:WIDTH] = x
                    else:
                        base[k, :, pl.ds(lo, BLOCK)] = x
                return prepare([lambda lo, last, x=x: x for x in values], lo, last)

            edges = prepare_all(r, body)
            loads = [kept(k) for k in range(4)]

        if r == 0:
            arrived(table_rows, tab_recv)
        arrived(first_a, a1_recv.at[r])
        second_a = relay_a(r)
        arrived(first_b, b1_recv.at[r])
        second_b = relay_b(r)

        if depth > 1:
            arrived(edges, e_recv.at[r])
        others(r, edges)
        bases = advance(r, loads)
        wm, u = adj

        arrived(second_a[0], a2_recv.at[r])
        if depth > 2:
            arrived(second_a[1], p2_recv.at[r])
        if r == 0:
            wet_h = opened_rows(merged(ha_r, 0, 5), 4)
        h_m, h_s = opened(ha_r, r)
        g_p = gained(opened_sums(ha_r, hp_r, r, shallower), [x[0:1] for x in bases[4]], wet_h)
        g_m, g_s = gained(h_m, state[0], wet_h), gained(h_s, state[1], wet_h)
        gain_m = [c * a + press * (running(b, True) + x) for c, a, b, x in zip(mdif_p, g_m, g_s, g_p)]
        gain_s = [c * a for c, a in zip(tdif_p, g_s)]
        if r == 0:
            m_p, s_p = spread(bases[0], gain_m), spread(bases[1], gain_s)
            first_a = send_p(1, gath_p[1], s_p)
            first_a += send_a(1, gath_a[1], m_p, s_p)
        if r == 1:
            arrived(sent[0], send_sem)
        arrived(second_b[0], b2_recv.at[r])
        if depth > 2:
            arrived(second_b[1], t2_recv.at[r])
        h_w, h_u = opened(hb_r, r)
        gain_lm = gained(h_w, wm, wet_h)
        g_t = gained(opened_sums(hb_r, ht_r, r, deeper), [x[1:2] for x in bases[4]], wet_h)
        gain_lt = [a + press * x for a, x in zip(gained(h_u, u, wet_h), g_t)]
        if r == 0:
            lm_p, lt_p = spread(bases[2], gain_lm), spread(bases[3], gain_lt)
            adj = adjoint(mdif_p, tdif_p, lm_p, lt_p)
            first_b = send_t(1, gath_t[1], lm_p)
            first_b += send_b(1, gath_b[1], *adj)
            state = [m_p, s_p, lm_p, lt_p]
        gains = [gain_m, gain_s, gain_lm, gain_lt]

    add_ends(gains)
    outs = (mom_out, tra_out, mgrad_out, tgrad_out)

    def finish(b, carry):
        lo = pl.multiple_of(b * BLOCK, LANES)
        for k, out in enumerate(outs):
            out[0, :, pl.ds(lo, BLOCK)] = filled(k, gains, lo, False)
        return carry

    lax.fori_loop(0, BLOCKS, finish, 0)
    for k, out in enumerate(outs):
        out[0, :, MAIN:CELLS] = filled(k, gains, MAIN, True)[:, :REST]


def write_out(*refs):
    sources, targets, sems = refs[:4], refs[4:8], refs[8]
    writes = [pltpu.make_async_copy(sources[k], targets[k], sems.at[k]) for k in range(4)]
    for copy in writes:
        copy.start()
    for copy in writes:
        copy.wait()


def solution(mesh):
    tiles, depth = mesh.shape["tiles"], mesh.shape["depth"]
    inner = max(k for k in range(1, tiles + 1) if tiles % k == 0 and k * k <= tiles)
    outer = tiles // inner

    def local(*args):
        rows = args[0].shape[1]
        dma = pltpu.SemaphoreType.DMA
        f32 = jnp.float32
        shape = jax.ShapeDtypeStruct(args[0].shape, f32)
        vmem = pl.BlockSpec(memory_space=pltpu.VMEM)
        hbm = pl.BlockSpec(memory_space=pltpu.MemorySpace.HBM)

        def strips(*lead):
            return pltpu.VMEM((*lead, rows, LANES), f32)

        def few(*lead):
            return pltpu.VMEM((*lead, 4, LANES), f32)

        bulk_rows = 2 * rows * (16 * (inner + outer) + depth * (inner + outer + WIDTH // LANES))

        results = pl.pallas_call(
            functools.partial(kernel, inner, outer, depth, rows * depth),
            out_shape=(pltpu.VMEM(shape.shape, f32),) * 4,
            in_specs=[hbm] * 11,
            out_specs=(vmem,) * 4,
            scratch_shapes=[
                pltpu.VMEM((7, *args[0].shape[1:]), f32),
                *[pltpu.VMEM(args[k].shape, args[k].dtype) for k in (5, 6, 7)],
                pltpu.SMEM(args[8].shape, jnp.int32),
                *[pltpu.VMEM((rows, WIDTH), f32)] * 4,
                pltpu.VMEM((5 * rows, GRID), f32),
                pltpu.VMEM((4, rows, WIDTH), f32),
                pltpu.VMEM((2, rows, WIDTH), f32),
                pltpu.VMEM((2, depth, rows, WIDTH), f32),
                strips(2, 6), strips(2, 5), few(2), few(2),
                strips(inner, 6), strips(inner, 6), strips(outer, 5), strips(outer, 5),
                few(inner), few(inner), few(outer), few(outer),
                strips(2, outer, 6), strips(2, inner, 6),
                strips(2, outer, 6), strips(2, inner, 6), strips(2, outer, depth), strips(2, inner, depth),
                pltpu.VMEM((1, LANES), jnp.int32),
                pltpu.VMEM((outer + inner - 1, 1, LANES), jnp.int32),
                pltpu.VMEM((bulk_rows, 1, LANES), f32),
                dma((7,)), dma(()), dma(()), *[dma((2,))] * 5, *[dma((2 if depth > 2 else 1,))] * 2,
            ],
            compiler_params=pltpu.CompilerParams(
                collective_id=0, has_side_effects=True, vmem_limit_bytes=62 * 1024 * 1024
            ),
        )(*args)
        return pl.pallas_call(
            write_out,
            out_shape=(shape,) * 4,
            in_specs=[vmem] * 4,
            out_specs=(hbm,) * 4,
            scratch_shapes=[dma((4,))],
            compiler_params=pltpu.CompilerParams(vmem_limit_bytes=62 * 1024 * 1024),
        )(*[pltpu.with_memory_space_constraint(x, pltpu.VMEM) for x in results])

    whole = P("tiles", "depth", None)
    flat = P("tiles", None)
    in_specs = (whole,) * 5 + (flat,) * 4 + (whole,) * 2
    return jax.shard_map(local, mesh=mesh, in_specs=in_specs, out_specs=(whole,) * 4, check_vma=False)
```

```python
import functools

import jax
import jax.numpy as jnp
from jax import lax
from jax.experimental import pallas as pl
from jax.experimental.pallas import tpu as pltpu
from jax.sharding import PartitionSpec as P

NI = 90
NJ = 70
CELLS = NI * NJ
LANES = 128
MAIN = 64 * NI
BLOCK = 5 * LANES
BLOCKS = MAIN // BLOCK
WIDTH = MAIN + BLOCK
REST = CELLS - MAIN
GRID = WIDTH + 2 * LANES
NORTH = NI * (NJ - 1) % LANES
HEAD = LANES - NI
SIX = NJ - 64
INVERSE = 37
MESH = pl.DeviceIdType.MESH


def roll(x, shift, axis=1):
    return pltpu.roll(x, shift % x.shape[axis], axis)


def pick(x, lanes):
    return jnp.take_along_axis(x, lanes & (LANES - 1), axis=1, mode="promise_in_bounds")


def kernel(
    inner, outer, depth, levels_all,
    mom_hbm, tra_hbm, mdif_hbm, tdif_hbm, mix_hbm, wet_hbm, nb_hbm, se_hbm, fl_hbm, mcot_hbm, tcot_hbm,
    mom_out, tra_out, mgrad_out, tgrad_out,
    fields, wet_ref, nb_ref, se_ref, fl_s, on_ref, ke_ref, kw_ref, wet8, grid, base, edge_s, edge_r,
    a_s, b_s, p_s, t_s, ga_0, ga_1, gb_0, gb_1, gp_0, gp_1, gt_0, gt_1, ha_s, hb_s, ha_r, hb_r, hp_r, ht_r,
    table, tables,
    bulk, in_sem, send_sem, tab_recv, e_recv, a1_recv, b1_recv, a2_recv, b2_recv, p2_recv, t2_recv,
):
    me = lax.axis_index("tiles")
    d = lax.axis_index("depth")
    member = lax.rem(me, inner)
    group = lax.div(me, inner)
    relay = depth - 1 - d
    rows = fields.shape[1]
    press = -0.1 * levels_all ** (-0.5)
    f32 = jnp.float32

    def partner(at, o, count):
        if count & (count - 1):
            return lax.rem(at + o, count)
        out = at
        for bit in [1 << k for k in range(count.bit_length()) if o >> k & 1]:
            out = out + bit - 2 * bit * lax.rem(lax.div(at, bit), 2)
        return out

    def back(o, count):
        return (count - o) % count if count & (count - 1) else o

    def in_inner(o, at):
        return {"tiles": group * inner + partner(member, o, inner), "depth": at}

    def in_outer(o, at):
        return {"tiles": partner(group, o, outer) * inner + member, "depth": at}

    far_first = sorted(range(outer), key=lambda o: (-(o & (outer // 2)), o == 0, o))
    far_inner = list(range(inner))[::-1]

    def shifted(o):
        return lax.rem(d + o, depth)

    barrier = pltpu.get_barrier_semaphore()
    greeted = [in_outer(o, shifted(k)) for o in range(outer) for k in range(depth) if o or k]
    greeted += [in_inner(o, at) for o in range(1, inner) for at in (d, relay)]
    for device in greeted:
        pl.semaphore_signal(barrier, inc=1, device_id=device, device_id_type=MESH)

    fetched = [pltpu.make_async_copy(nb_hbm, nb_ref, in_sem.at[0]), pltpu.make_async_copy(se_hbm, se_ref, in_sem.at[1])]
    fetched.append(pltpu.make_async_copy(fl_hbm, fl_s, in_sem.at[2]))
    fetched.append(pltpu.make_async_copy(wet_hbm, wet_ref, in_sem.at[3]))
    parts = ((0, 2), (2, 6), (6, 7))
    for k, src in enumerate((mom_hbm, tra_hbm, mcot_hbm, mdif_hbm, tcot_hbm, tdif_hbm, mix_hbm)):
        group_of = [n for n, (a, b) in enumerate(parts) if a <= k < b][0]
        fetched.append(pltpu.make_async_copy(src, fields.at[pl.ds(k, 1)], in_sem.at[4 + group_of]))
    for copy in fetched:
        copy.start()

    def fields_in(n):
        part = fields.at[pl.ds(parts[n][0], parts[n][1] - parts[n][0])]
        pltpu.make_async_copy(part, part, in_sem.at[4 + n]).wait()

    sent = [0]

    def size(ref):
        count = 1
        for n in ref.shape:
            count *= n
        return count // LANES

    def send(src, dst, rsem, to):
        pltpu.make_async_remote_copy(
            src_ref=src, dst_ref=dst, send_sem=send_sem, recv_sem=rsem, device_id=to, device_id_type=MESH
        ).start()
        sent[0] += size(dst)
        assert sent[0] <= bulk.shape[0]
        return size(dst)

    def arrived(count, sem):
        part = bulk.at[pl.ds(0, count)]
        pltpu.make_async_copy(part, part, sem).wait()


    lane = lax.broadcasted_iota(jnp.int32, (rows, LANES), 1)
    sub = lax.broadcasted_iota(jnp.int32, (rows, LANES), 0)
    level = lax.broadcasted_iota(jnp.int32, (rows, BLOCK), 0)
    place = lax.broadcasted_iota(jnp.int32, (rows, BLOCK), 1).astype(f32)
    odd = (lane & 1) == 1
    i_n = (lane + LANES - NORTH) & (LANES - 1)
    i_s = lane
    j_m = (jnp.where(odd, (lane + LANES - NI + 1) >> 1, lane >> 1) * INVERSE) & 63
    j_t = jnp.full_like(lane, -1)
    for j in range(64, NJ):
        for x in (NI * j % LANES, (NI * j + NI - 1) % LANES):
            j_t = jnp.where(lane == x, j, j_t)
    is_t = j_t >= 0
    corner_s = (lane == 0) | (lane == NI - 1)
    corner_n = (lane == NORTH) | (lane == (NORTH + NI - 1) % LANES)

    zero = jnp.zeros((5 * rows, LANES), f32)
    grid[:, 0:LANES] = zero
    grid[:, GRID - 2 * LANES : GRID - LANES] = zero
    grid[:, GRID - LANES :] = zero
    table[...] = jnp.zeros_like(table)

    def marks(b, carry):
        lo = pl.multiple_of(b * BLOCK, LANES)
        pos = place + lo.astype(f32)
        col = pos - NI * jnp.floor((pos + 0.5) * (1.0 / NI))
        inside = pos < CELLS - 0.5
        west = (col < 0.5) & inside
        east = (col > NI - 1.5) & inside
        on_ref[:, pl.ds(lo, BLOCK)] = jnp.where(west | east, 1.0, 0.0)
        ke_ref[:, pl.ds(lo, BLOCK)] = jnp.where(east, 0.0, 1.0)
        kw_ref[:, pl.ds(lo, BLOCK)] = jnp.where(west, 0.0, 1.0)
        return carry

    lax.fori_loop(0, BLOCKS + 1, marks, 0)

    for copy in fetched[:3]:
        copy.wait()
    table[:, 0:4] = nb_ref[...]
    table[:, 4:8] = se_ref[...]
    pl.semaphore_wait(barrier, len(greeted))
    table_rows = sum(
        send(table, tables.at[k], tab_recv, to)
        for k, to in [(o, in_outer(o, relay)) for o in far_first]
        + [(outer + o - 1, in_inner(o, relay)) for o in far_inner if o]
    )
    flip = [fl_s[0, k] for k in range(4)]
    f_ew = jnp.where(odd, flip[2], flip[3])
    i_n = i_n + flip[0] * (NI - 1 - 2 * i_n)
    i_s = i_s + flip[1] * (NI - 1 - 2 * i_s)
    j_m = j_m + f_ew * (NJ - 1 - 2 * j_m)
    j_t = j_t + f_ew * (NJ - 1 - 2 * j_t)
    m_main, t_main = j_m < 64, j_t < 64
    shift = jnp.where(odd, 0, NI - 1)
    m_from, t_from = NI * j_m + shift, NI * j_t + shift
    shift = jnp.where(odd, NI - HEAD, LANES - 2 * SIX) - 64
    m_rest, t_rest = j_m + shift, j_t + shift

    def padded(x):
        return jnp.concatenate([x, jnp.zeros((x.shape[0], BLOCK - REST), x.dtype)], axis=1)

    def field(k):
        def load(lo, last):
            return padded(fields[k, :, MAIN:CELLS]) if last else fields[k, :, pl.ds(lo, BLOCK)]
        return load

    def kept(k):
        def load(lo, last):
            return base[k, :, MAIN:WIDTH] if last else base[k, :, pl.ds(lo, BLOCK)]
        return load

    def wide(ref):
        def load(lo, last):
            return ref[:, MAIN:WIDTH] if last else ref[:, pl.ds(lo, BLOCK)]
        return load

    def wet_int(lo, last):
        x = padded(wet_ref[0:1, MAIN:CELLS]) if last else wet_ref[0:1, pl.ds(lo, BLOCK)]
        return jnp.broadcast_to(x.astype(f32), (rows, BLOCK))

    mdif, tdif, mix = field(3), field(5), field(6)
    on, keep_e, keep_w, wet_at = wide(on_ref), wide(ke_ref), wide(kw_ref), wide(wet8)

    def cut(x, c):
        return x[:, c * LANES : (c + 1) * LANES]

    def collect(acc, x, mask):
        for c in range(BLOCK // LANES):
            acc = jnp.where(cut(mask, c) > 0.5, cut(x, c), acc)
        return acc

    def sweep(body, count):
        def step(b, accs):
            lo = pl.multiple_of(b * BLOCK, LANES)
            mask = on(lo, False)
            return tuple(collect(a, x, mask) for a, x in zip(accs, body(lo, False)))
        accs = lax.fori_loop(0, BLOCKS, step, (jnp.zeros((rows, LANES), f32),) * count)
        mask = on(MAIN, True)
        ends = body(MAIN, True)
        tails = [collect(jnp.zeros((rows, LANES), f32), x, mask) for x in ends]
        norths = [jnp.where(lane >= NORTH, cut(x, 3), cut(x, 4)) for x in ends]
        return norths, accs, tails

    def running(x, down):
        at = lax.broadcasted_iota(jnp.int32, x.shape, 0)
        k = 1
        while k < rows:
            if down:
                x = x + jnp.where(at >= k, roll(x, k, 0), 0.0)
            else:
                x = x + jnp.where(at < rows - k, roll(x, rows - k, 0), 0.0)
            k *= 2
        return x

    def total(x):
        k = rows // 2
        while k >= 1:
            x = x + roll(x, k, 0)
            k //= 2
        return x

    def packed(refs, masked):
        sources = [field(r) for r in refs]

        def body(lo, last):
            values = [load(lo, last) for load in sources]
            if masked:
                values.append(wet_int(lo, last))
                if last:
                    wet8[:, MAIN:WIDTH] = values[-1]
                else:
                    wet8[:, pl.ds(lo, BLOCK)] = values[-1]
            return values

        norths, accs, tails = sweep(body, len(refs) + masked)
        souths = [fields[k, :, 0:LANES] for k in refs] + [wet8[:, 0:LANES]] * masked
        return [list(p) for p in zip(norths, souths, accs, tails)]

    fetched[3].wait()
    fields_in(0)
    m_p, s_p, wet_p = packed([0, 1], 1)
    wet_p[0] = jnp.where((lane >= NORTH) | (lane < NORTH + NI - LANES), wet_p[0], 0.0)
    wet_p[1] = jnp.where(lane < NI, wet_p[1], 0.0)
    wet_p[3] = jnp.where(is_t, wet_p[3], 0.0)

    t_lane = jnp.where(lane < 64, lane - (NI - HEAD), lane - (LANES - 2 * SIX))
    t_lane = jnp.where(t_lane >= SIX, t_lane - SIX, t_lane)
    t_lane = NI * (64 + t_lane) + jnp.where(lane < 64, 0, NI - 1)
    second = ((lane < 64) & (lane >= NI - HEAD + SIX)) | (lane >= LANES - SIX)

    def put(ref, r, one, two):
        n2, s2 = roll(two[0], NI - NORTH), roll(two[1], NI)
        ref[r, 0] = jnp.where(lane < NI, roll(one[0], -NORTH), n2)
        ref[r, 1] = jnp.where(lane < NI, one[1], s2)
        ends = jnp.where(second, pick(two[3], t_lane), pick(one[3], t_lane))
        ref[r, 2] = jnp.where(
            lane < NI - HEAD, n2,
            jnp.where((lane >= 64) & (lane < LANES - 2 * SIX), roll(two[1], 64 - HEAD), ends),
        )
        ref[r, 3] = one[2]
        ref[r, 4] = two[2]

    def sums(packs):
        n, s, ew, tl = [total(x * w) for x, w in zip(packs, wet_p)]
        n = roll(n, -NORTH)
        out = jnp.where(sub == 0, n, jnp.where(sub == 1, s, jnp.where(sub == 2, ew, tl)))
        return out[0:4]

    def send_p(r, gath, s_p):
        p_s[r] = gath[member] = sums(s_p)
        return sum(send(p_s.at[r], gath.at[member], a1_recv.at[r], in_inner(o, d)) for o in far_inner if o)

    def send_t(r, gath, lm_p):
        t_s[r] = gath[group] = sums(lm_p)
        return sum(send(t_s.at[r], gath.at[group], b1_recv.at[r], in_outer(o, d)) for o in far_first if o)

    def send_a(r, gath, m_p, s_p):
        put(a_s, r, [x * w for x, w in zip(m_p, wet_p)], [x * w for x, w in zip(s_p, wet_p)])
        if r == 0:
            out = jnp.where(sub == 4, roll(wet_p[0], -NORTH), 0.0)
            for k in range(1, 4):
                out = jnp.where(sub == 4 + k, wet_p[k], out)
            a_s[r, 5] = out
        span = pl.ds(0, 6 - r)
        return sum(
            send(a_s.at[r, span], gath.at[member, span], a1_recv.at[r], in_inner(o, relay))
            for o in far_inner
        )

    def adjoint(mdif_p, tdif_p, lm_p, lt_p):
        wm = [a * b for a, b in zip(mdif_p, lm_p)]
        u = [a * b + press * running(c, False) for a, b, c in zip(tdif_p, lt_p, lm_p)]
        return wm, u

    def send_b(r, gath, wm, u):
        put(b_s, r, [x * w for x, w in zip(wm, wet_p)], [x * w for x, w in zip(u, wet_p)])
        return sum(send(b_s.at[r], gath.at[group], b1_recv.at[r], in_outer(o, relay)) for o in far_first)

    gath_a, gath_b, gath_p, gath_t = (ga_0, ga_1), (gb_0, gb_1), (gp_0, gp_1), (gt_0, gt_1)

    first_a = send_p(0, gath_p[0], s_p)
    first_a += send_a(0, gath_a[0], m_p, s_p)
    fields_in(1)
    lm_p, mdif_p, lt_p, tdif_p = packed([2, 3, 4, 5], 0)
    state = [m_p, s_p, lm_p, lt_p]
    first_b = send_t(0, gath_t[0], lm_p)
    adj = adjoint(mdif_p, tdif_p, lm_p, lt_p)
    first_b += send_b(0, gath_b[0], *adj)
    fields_in(2)

    routes = {}

    def route(o, across):
        if (o, across) not in routes:
            if across:
                slot = outer + back(o, inner) - 1 if o else 0
            else:
                slot = back(o, outer)
            found = []
            for k in range(4):
                tile = tables[slot, 0, k]
                edge = tables[slot, 0, 4 + k]
                known = jnp.maximum(tile, 0)
                its_group, its_member = lax.div(known, inner), lax.rem(known, inner)
                if across:
                    here, spot = its_member == member, its_group
                else:
                    here, spot = its_group == group, its_member
                found.append((spot, edge, jnp.where((tile >= 0) & here, 1.0, 0.0)))
            routes[o, across] = found
        return routes[o, across]

    def either(x, turned, straight):
        return x * straight + turned * (1.0 - straight)

    def relayed(gath, o, across):
        (tn, en, hn), (ts, es, hs), (te, ee, he), (tw, ew, hw) = route(o, across)
        en, es = jnp.where(en == 0, 0, 1), jnp.where(es == 0, 0, 1)
        fn, fs = 1.0 - en.astype(f32), es.astype(f32)
        fe, fw = jnp.where(ee == 3, 1.0, 0.0), jnp.where(ew == 2, 1.0, 0.0)
        v_n = gath[tn, en] * hn
        v_s = gath[ts, es] * hs
        x_n, x_s, x_e, x_w = gath[tn, 2] * hn, gath[ts, 2] * hs, gath[te, 2] * he, gath[tw, 2] * hw
        x_n, x_s = either(x_n, roll(x_n, 64), fn), either(x_s, roll(x_s, 64), fs)
        x_e, x_w = either(x_e, roll(x_e, 64), fe), either(x_w, roll(x_w, 64), fw)
        v_r = jnp.where(
            lane < 64, jnp.where(lane < NI - HEAD, x_n, x_e), jnp.where(lane < LANES - 2 * SIX, x_s, x_w)
        )
        sides = []
        for k in (3, 4):
            e, w = gath[te, k] * he, gath[tw, k] * hw
            sides.append(jnp.where(odd, either(w, roll(w, NI - 1), fw), either(e, roll(e, 1 - NI), fe)))
        return [v_n, v_s, v_r] + sides

    def relayed_rows(load, o, across):
        (tn, en, hn), (ts, es, hs), (te, ee, he), (tw, ew, hw) = route(o, across)
        at = sub & 3
        fn, fs = jnp.where(en == 0, 1.0, 0.0), jnp.where(es == 0, 0.0, 1.0)
        fe, fw = jnp.where(ee == 3, 1.0, 0.0), jnp.where(ew == 2, 1.0, 0.0)
        n, s, e, w = load(tn) * hn, load(ts) * hs, load(te) * he, load(tw) * hw
        n, s = either(n, roll(n, -1, 0), fn), either(s, roll(s, 1, 0), fs)
        e, w = either(e, roll(e, 1 - NI), fe), either(w, roll(w, NI - 1), fw)
        return jnp.where(at == 0, n, jnp.where(at == 1, s, jnp.where(odd, w, e)))

    def rows_at(ref, t):
        x = ref[t]
        return jnp.concatenate([x, x], axis=0)

    def to_depths(src, dst, r, o, rsem, place):
        return sum(send(src, dst.at[r, o, k], rsem.at[r], place(o, shifted(k))) for k in range(1, depth) if depth > 2)

    def relay_a(r):
        for o in far_first:
            out = relayed(gath_a[r], o, False)
            if r == 0:
                load = lambda t: jnp.where(sub < 4, rows_at(gath_p[0], t), gath_a[0][t, 5])
            else:
                load = lambda t: rows_at(gath_p[1], t)
            out.append(relayed_rows(load, o, False))
            for k, x in enumerate(out):
                ha_s[r, o, k] = x
        count = extra = 0
        for o in far_first:
            count += send(ha_s.at[r, o], ha_r.at[r, o], a2_recv.at[r], in_outer(o, relay))
            extra += to_depths(ha_s.at[r, o, 5], hp_r, r, o, p2_recv, in_outer)
        return count, extra

    def relay_b(r):
        spots = far_inner
        for o in spots:
            out = relayed(gath_b[r], o, True)
            out.append(relayed_rows(lambda t: rows_at(gath_t[r], t), o, True))
            for k, x in enumerate(out):
                hb_s[r, o, k] = x
        count = extra = 0
        for o in spots:
            count += send(hb_s.at[r, o], hb_r.at[r, o], b2_recv.at[r], in_inner(o, relay))
            extra += to_depths(hb_s.at[r, o, 5], ht_r, r, o, t2_recv, in_inner)
        return count, extra

    def prepare(loads, lo, last):
        m, s, lm, lt = [load(lo, last) for load in loads]
        w = wet_at(lo, last)
        mixed = mix(lo, last) * lt
        back = running(lm, False)
        at = slice(LANES + MAIN, LANES + WIDTH) if last else pl.ds(pl.multiple_of(lo + LANES, LANES), BLOCK)
        grid[0:rows, at] = w * m
        grid[rows : 2 * rows, at] = w * s
        grid[3 * rows : 4 * rows, at] = w * (mdif(lo, last) * lm)
        grid[4 * rows : 5 * rows, at] = w * (tdif(lo, last) * lt + press * back)
        out = jnp.where(level == 0, s, total(s))
        out = jnp.where(level == 1, roll(mixed, 1, 0), out)
        out = jnp.where(level == 2, roll(back, 2, 0), out)
        out = jnp.where(level == 3, roll(s, 4, 0), out)
        out = jnp.where(level == 4, roll(mixed, 5, 0), out)
        return out

    def prepare_all(r, body):
        def step(b, carry):
            lo = pl.multiple_of(b * BLOCK, LANES)
            edge_s[r, :, pl.ds(lo, BLOCK)] = body(lo, False)
            return carry
        lax.fori_loop(0, BLOCKS, step, 0)
        edge_s[r, :, MAIN:WIDTH] = body(MAIN, True)
        return sum(
            send(edge_s.at[r], edge_r.at[r, o], e_recv.at[r], {"tiles": me, "depth": shifted(o)})
            for o in range(1, depth)
        )

    def origin(o):
        return lax.rem(d + depth - o, depth)

    shallower = [None] + [jnp.where(origin(o) < d, 1.0, 0.0) for o in range(1, depth)]
    deeper = [None] + [jnp.where(origin(o) > d, 1.0, 0.0) for o in range(1, depth)]
    has_above = jnp.where(d > 0, 1.0, 0.0)
    has_below = jnp.where(d < depth - 1, 1.0, 0.0)

    def others(r, edges):
        def body(lo, last):
            w = wet_at(lo, last)
            out = jnp.where(level == 2, w, 0.0)
            for o in range(1, depth):
                x = edge_r[r, o, :, MAIN:WIDTH] if last else edge_r[r, o, :, pl.ds(lo, BLOCK)]
                x = x * w
                out = out + jnp.where(level == 0, roll(x, -5, 0) * shallower[o], 0.0)
                out = out + jnp.where(level == 1, roll(x, -1, 0) * deeper[o], 0.0)
            at = slice(LANES + MAIN, LANES + WIDTH) if last else pl.ds(pl.multiple_of(lo + LANES, LANES), BLOCK)
            grid[2 * rows : 3 * rows, at] = out

        def step(b, carry):
            body(pl.multiple_of(b * BLOCK, LANES), False)
            return carry

        if depth > 1:
            lax.fori_loop(0, BLOCKS, step, 0)
            body(MAIN, True)

    def advance(r, loads):
        def around(g, lo, last, e, w):
            span = slice(g * rows, (g + 1) * rows)
            x = grid[span, MAIN:GRID] if last else grid[span, pl.ds(lo, BLOCK + 2 * LANES)]
            def at(k):
                return roll(x, -k)[:, LANES : LANES + BLOCK]
            return at(NI) + at(-NI) + at(1) * e + at(-1) * w, x[:, LANES : LANES + BLOCK]

        def body(lo, last):
            e, w, wet = keep_e(lo, last), keep_w(lo, last), wet_at(lo, last)
            sums, own_x = around(2, lo, last, e, w)
            weights = sums[2:3]
            lap_x = wet * sums - weights * own_x
            def lap(g):
                sums, own = around(g, lo, last, e, w)
                return wet * sums - weights * own
            m, s, lm, lt = [load(lo, last) for load in loads]
            mx = mix(lo, last)
            mixed = mx * lt

            def vertical(q, which):
                above, below = q[0:1], q[rows - 1 : rows]
                if depth > 1:
                    x = edge_r[r, 1, :, MAIN:WIDTH] if last else edge_r[r, 1, :, pl.ds(lo, BLOCK)]
                    y = x if depth == 2 else (
                        edge_r[r, depth - 1, :, MAIN:WIDTH] if last else edge_r[r, depth - 1, :, pl.ds(lo, BLOCK)]
                    )
                    above = x[3 + which : 4 + which] * has_above + above * (1.0 - has_above)
                    below = y[which : which + 1] * has_below + below * (1.0 - has_below)
                up = jnp.where(level == 0, above, roll(q, 1, 0))
                down = jnp.where(level == rows - 1, below, roll(q, rows - 1, 0))
                return (up - q) + (down - q)

            lap_s = lap(1)
            results = [
                m + mdif(lo, last) * lap(0) + press * (running(lap_s, True) + lap_x[0:1]),
                s + tdif(lo, last) * lap_s + mx * vertical(s, 0) + 0.2 * m,
                lm + lap(3) + 0.2 * lt,
                lt + vertical(mixed, 1) + lap(4) + press * lap_x[1:2],
            ]
            for k, x in enumerate(results):
                if last:
                    base[k, :, MAIN:WIDTH] = x
                else:
                    base[k, :, pl.ds(lo, BLOCK)] = x
            return results + [own_x]

        norths, accs, tails = sweep(body, 5)
        souths = [base[k, :, 0:LANES] for k in range(4)] + [grid[2 * rows : 3 * rows, LANES : 2 * LANES]]
        return [list(p) for p in zip(norths, souths, accs, tails)]

    def merged(ref, r, k):
        out = ref[r, 0, k]
        for o in range(1, ref.shape[1]):
            out = out + ref[r, o, k]
        return out

    def opened(ref, r):
        v_n, v_s, v_r, e_1, e_2 = [merged(ref, r, k) for k in range(5)]
        one = [pick(v_n, i_n), pick(v_s, i_s)]
        two = [
            jnp.where(i_n < HEAD, pick(v_n, NI + i_n), pick(v_r, i_n - HEAD)),
            jnp.where(i_s < HEAD, pick(v_s, NI + i_s), pick(v_r, 64 + i_s - HEAD)),
        ]
        for k, (out, e) in enumerate(((one, e_1), (two, e_2))):
            out.append(jnp.where(m_main, pick(e, m_from), pick(v_r, m_rest + SIX * k)))
            out.append(jnp.where(t_main, pick(e, t_from), pick(v_r, t_rest + SIX * k)))
        return one, two

    def opened_rows(x, k):
        ew, tl = pick(x, m_from), pick(x, t_from)
        rows_of = [
            pick(x, i_n)[k : k + 1], pick(x, i_s)[k + 1 : k + 2],
            jnp.where(m_main, ew[k + 2 : k + 3], ew[k + 3 : k + 4]),
            jnp.where(t_main, tl[k + 2 : k + 3], tl[k + 3 : k + 4]),
        ]
        return [jnp.broadcast_to(y, (rows, LANES)) for y in rows_of]

    def opened_sums(attached, apart, r, gates):
        if depth == 2:
            x = merged(attached, r, 5) * gates[1]
        else:
            x = jnp.zeros((rows, LANES), f32)
            for k in range(1, depth):
                for o in range(apart.shape[1]):
                    x = x + apart[r, o, k] * gates[k]
        return opened_rows(x, 0)

    def gained(halo, own, wet_h):
        return [w * (h - v * q) for w, h, v, q in zip(wet_p, halo, wet_h, own)]

    def spread(old, gain):
        n, s, ew, tl = gain
        return [
            old[0] + n + jnp.where(corner_n, tl, 0.0),
            old[1] + s + jnp.where(corner_s, ew, 0.0),
            old[2] + ew + jnp.where(corner_s, s, 0.0),
            old[3] + tl + jnp.where(corner_n, n, 0.0),
        ]

    def add_ends(gains):
        for k in range(4):
            base[k, :, 0:LANES] = base[k, :, 0:LANES] + gains[k][1]
            at = slice(MAIN + 3 * LANES, MAIN + 4 * LANES)
            base[k, :, at] = base[k, :, at] + jnp.where(lane >= NORTH, gains[k][0], 0.0)
            at = slice(MAIN + 4 * LANES, WIDTH)
            base[k, :, at] = base[k, :, at] + jnp.where(lane < NORTH + NI - LANES, gains[k][0], 0.0)

    def filled(k, gains, lo, last):
        side = jnp.concatenate([gains[k][3 if last else 2]] * (BLOCK // LANES), axis=1)
        return kept(k)(lo, last) + on(lo, last) * side

    loads = [field(k) for k in (0, 1, 2, 4)]
    wet_h = gains = None
    for r in range(2):
        if r == 0:
            edges = prepare_all(r, functools.partial(prepare, loads))
        else:
            add_ends(gains)

            def body(lo, last):
                values = [filled(k, gains, lo, last) for k in range(4)]
                for k, x in enumerate(values):
                    if last:
                        base[k, :, MAIN:WIDTH] = x
                    else:
                        base[k, :, pl.ds(lo, BLOCK)] = x
                return prepare([lambda lo, last, x=x: x for x in values], lo, last)

            edges = prepare_all(r, body)
            loads = [kept(k) for k in range(4)]

        if r == 0:
            arrived(table_rows, tab_recv)
        if r == 0:
            for o in far_first:
                route(o, False)
            for o in range(inner):
                route(o, True)
        arrived(first_a, a1_recv.at[r])
        second_a = relay_a(r)
        arrived(first_b, b1_recv.at[r])
        second_b = relay_b(r)

        if depth > 1:
            arrived(edges, e_recv.at[r])
        others(r, edges)
        bases = advance(r, loads)
        wm, u = adj

        arrived(second_a[0], a2_recv.at[r])
        if depth > 2:
            arrived(second_a[1], p2_recv.at[r])
        if r == 0:
            wet_h = opened_rows(merged(ha_r, 0, 5), 4)
        h_m, h_s = opened(ha_r, r)
        g_p = gained(opened_sums(ha_r, hp_r, r, shallower), [x[0:1] for x in bases[4]], wet_h)
        g_m, g_s = gained(h_m, state[0], wet_h), gained(h_s, state[1], wet_h)
        gain_m = [c * a + press * (running(b, True) + x) for c, a, b, x in zip(mdif_p, g_m, g_s, g_p)]
        gain_s = [c * a for c, a in zip(tdif_p, g_s)]
        if r == 0:
            m_p, s_p = spread(bases[0], gain_m), spread(bases[1], gain_s)
            first_a = send_p(1, gath_p[1], s_p)
            first_a += send_a(1, gath_a[1], m_p, s_p)
        if r == 1:
            arrived(sent[0], send_sem)
        arrived(second_b[0], b2_recv.at[r])
        if depth > 2:
            arrived(second_b[1], t2_recv.at[r])
        h_w, h_u = opened(hb_r, r)
        gain_lm = gained(h_w, wm, wet_h)
        g_t = gained(opened_sums(hb_r, ht_r, r, deeper), [x[1:2] for x in bases[4]], wet_h)
        gain_lt = [a + press * x for a, x in zip(gained(h_u, u, wet_h), g_t)]
        if r == 0:
            lm_p, lt_p = spread(bases[2], gain_lm), spread(bases[3], gain_lt)
            adj = adjoint(mdif_p, tdif_p, lm_p, lt_p)
            first_b = send_t(1, gath_t[1], lm_p)
            first_b += send_b(1, gath_b[1], *adj)
            state = [m_p, s_p, lm_p, lt_p]
        gains = [gain_m, gain_s, gain_lm, gain_lt]

    add_ends(gains)
    outs = (mom_out, tra_out, mgrad_out, tgrad_out)

    def finish(b, carry):
        lo = pl.multiple_of(b * BLOCK, LANES)
        for k, out in enumerate(outs):
            out[0, :, pl.ds(lo, BLOCK)] = filled(k, gains, lo, False)
        return carry

    lax.fori_loop(0, BLOCKS, finish, 0)
    for k, out in enumerate(outs):
        out[0, :, MAIN:CELLS] = filled(k, gains, MAIN, True)[:, :REST]


def write_out(*refs):
    sources, targets, sems = refs[:4], refs[4:8], refs[8]
    writes = [pltpu.make_async_copy(sources[k], targets[k], sems.at[k]) for k in range(4)]
    for copy in writes:
        copy.start()
    for copy in writes:
        copy.wait()


def solution(mesh):
    tiles, depth = mesh.shape["tiles"], mesh.shape["depth"]
    inner = max(k for k in range(1, tiles + 1) if tiles % k == 0 and k * k <= tiles)
    outer = tiles // inner

    def local(*args):
        rows = args[0].shape[1]
        dma = pltpu.SemaphoreType.DMA
        f32 = jnp.float32
        shape = jax.ShapeDtypeStruct(args[0].shape, f32)
        vmem = pl.BlockSpec(memory_space=pltpu.VMEM)
        hbm = pl.BlockSpec(memory_space=pltpu.MemorySpace.HBM)

        def strips(*lead):
            return pltpu.VMEM((*lead, rows, LANES), f32)

        def few(*lead):
            return pltpu.VMEM((*lead, 4, LANES), f32)

        bulk_rows = 2 * rows * (16 * (inner + outer) + depth * (inner + outer + WIDTH // LANES))

        results = pl.pallas_call(
            functools.partial(kernel, inner, outer, depth, rows * depth),
            out_shape=(pltpu.VMEM(shape.shape, f32),) * 4,
            in_specs=[hbm] * 11,
            out_specs=(vmem,) * 4,
            scratch_shapes=[
                pltpu.VMEM((7, *args[0].shape[1:]), f32),
                *[pltpu.VMEM(args[k].shape, args[k].dtype) for k in (5, 6, 7)],
                pltpu.SMEM(args[8].shape, jnp.int32),
                *[pltpu.VMEM((rows, WIDTH), f32)] * 4,
                pltpu.VMEM((5 * rows, GRID), f32),
                pltpu.VMEM((4, rows, WIDTH), f32),
                pltpu.VMEM((2, rows, WIDTH), f32),
                pltpu.VMEM((2, depth, rows, WIDTH), f32),
                strips(2, 6), strips(2, 5), few(2), few(2),
                strips(inner, 6), strips(inner, 6), strips(outer, 5), strips(outer, 5),
                few(inner), few(inner), few(outer), few(outer),
                strips(2, outer, 6), strips(2, inner, 6),
                strips(2, outer, 6), strips(2, inner, 6), strips(2, outer, depth), strips(2, inner, depth),
                pltpu.VMEM((1, LANES), jnp.int32),
                pltpu.VMEM((outer + inner - 1, 1, LANES), jnp.int32),
                pltpu.VMEM((bulk_rows, 1, LANES), f32),
                dma((7,)), dma(()), dma(()), *[dma((2,))] * 5, *[dma((2 if depth > 2 else 1,))] * 2,
            ],
            compiler_params=pltpu.CompilerParams(
                collective_id=0, has_side_effects=True, vmem_limit_bytes=62 * 1024 * 1024
            ),
        )(*args)
        return pl.pallas_call(
            write_out,
            out_shape=(shape,) * 4,
            in_specs=[vmem] * 4,
            out_specs=(hbm,) * 4,
            scratch_shapes=[dma((4,))],
            compiler_params=pltpu.CompilerParams(vmem_limit_bytes=62 * 1024 * 1024),
        )(*[pltpu.with_memory_space_constraint(x, pltpu.VMEM) for x in results])

    whole = P("tiles", "depth", None)
    flat = P("tiles", None)
    in_specs = (whole,) * 5 + (flat,) * 4 + (whole,) * 2
    return jax.shard_map(local, mesh=mesh, in_specs=in_specs, out_specs=(whole,) * 4, check_vma=False)
```
